32 devices in a mesh: dp: 4 (over z), dom: 8 (over y, x, core).
Axes of the slice: x: 2, y: 2, z: 4, core: 2. Of those that a mesh axis runs over, the one named last changes fastest.
Arguments:
- feats: bfloat16 [4096, 1024], P(('dp', 'dom')), parts along dimension 0, may hold values from -26 to 26
- adj_own: int32 [4096, 128], P(('dp', 'dom')), parts along dimension 0, may hold values 0 or 1
- adj_prev: int32 [4096, 32], P(('dp', 'dom')), parts along dimension 0, may hold values 0 or 1
- adj_next: int32 [4096, 32], P(('dp', 'dom')), parts along dimension 0, may hold values 0 or 1
- bcount: int32 [32, 2], P('dp'), parts along dimension 0, may hold values from 1 to 32
- wqkv: bfloat16 [3, 1024, 1024], P(None, None, 'dom'), may hold values from -1 to 1, as said below
- w_mp: bfloat16 [1024, 1024], P('dom'), may hold values from -0.1875 to 0.1875
- w_out: bfloat16 [1024, 1024], P('dom'), may hold values from -0.1875 to 0.1875
Outputs:
- updated: bfloat16 [4096, 1024], P(('dp', 'dom')), parts along dimension 0
The draws below stay inside these ranges and needn't reach their ends.
There are 4 independent parts, one for each index of `dp`. The reference program is written for one: setup_inputs(seed, part) draws one part's arguments, and reference() takes and returns one part's arrays. A program takes and returns all parts, laid end to end along the dimension named above; an argument that names none is the same for every part. Nothing has to cross between parts.
Inputs may be any that keep to these rules, and one draw needn't show every extreme that they name: `wqkv`: projection weights with entries of deviation about 1024 ** -0.5.
All inputs are finite; a program needn't handle non-finite values. No bound on the sum of `adj_own` or of `adj_prev` or of `adj_next` on one device may be relied on, other than what follows from the above.
Results may differ from the reference program's by a relative error of at most 0.0066.
Values may be sent and summed in bfloat16 or wider, within the bound.
A program may use at most 64 MiB of HBM per device.

```python
import jax
import jax.numpy as jnp
from jax import lax

D = 1024
HEADS = 32
NODE_DEV = 128
BND = 32
NODES = 1024
N_DOM = 8


def draw_feats(key, part):
    first = jax.random.fold_in(key, 0)
    base = jnp.clip(jax.random.normal(first, (NODES, D), jnp.float32), -5.0, 5.0)
    return base.astype(jnp.bfloat16)


def draw_wqkv(key, part):
    base = jnp.clip(jax.random.normal(key, (3, D, D), jnp.float32), -4.0, 4.0) / D ** 0.5
    return base.astype(jnp.bfloat16)


def set_ends(result, key, smallest, high):
    place = [jax.random.randint(jax.random.fold_in(key, axis), (), 0, length) for axis, length in enumerate(result.shape)]
    longest = result.shape.index(max(result.shape))
    next_to = place[:longest] + [(place[longest] + 1) % result.shape[longest]] + place[longest + 1:]
    return result.at[tuple(place)].set(smallest).at[tuple(next_to)].set(high)


def levels(key, dims, cuts, smallest, high):
    loudness = 1.0
    for dim, parts in cuts:
        steps = jax.random.uniform(jax.random.fold_in(jax.random.fold_in(key, 6), dim), (parts,), jnp.float32, smallest / len(cuts), high / len(cuts))
        loudness = loudness * jnp.repeat(jnp.exp(steps), dims[dim] // parts).reshape((-1,) + (1,) * (len(dims) - 1 - dim))
    return loudness


def scatter_about(rng, shape, deviation, reach, cuts=(), kind=jnp.bfloat16):
    drawn = deviation * jax.random.normal(rng, shape, jnp.float32)
    if cuts:
        drawn = drawn * levels(rng, shape, cuts, -0.22, 0.18)
    return jnp.clip(drawn, -reach, reach).astype(kind)


def setup_inputs(seed: int = 0, part: int = 0) -> dict:
    streams_of = jax.random.split(jax.random.key(seed), 9)
    own_keys = jax.random.split(jax.random.fold_in(streams_of[8], part), 9)
    feats = draw_feats(jax.random.fold_in(jax.random.fold_in(streams_of[8], part), 71), part)
    adj_own = set_ends((jax.random.randint(own_keys[1], (NODES, NODE_DEV), 0, 24) < 1).astype(jnp.int32), jax.random.fold_in(own_keys[1], 1), 0, 1)
    adj_prev = set_ends((jax.random.randint(own_keys[2], (NODES, BND), 0, 6) < 1).astype(jnp.int32), jax.random.fold_in(own_keys[2], 1), 0, 1)
    adj_next = set_ends((jax.random.randint(own_keys[3], (NODES, BND), 0, 6) < 1).astype(jnp.int32), jax.random.fold_in(own_keys[3], 1), 0, 1)
    bcount = set_ends(jax.random.randint(own_keys[4], (N_DOM, 2), 1, BND + 1), jax.random.fold_in(own_keys[4], 1), 1, BND).astype(jnp.int32)
    wqkv = draw_wqkv(jax.random.fold_in(streams_of[8], 71), part)
    w_mp = scatter_about(streams_of[6], (D, D), D ** -0.5, 0.1875, ((0, 8),))
    w_out = scatter_about(streams_of[7], (D, D), D ** -0.5, 0.1875, ((0, 8),))
    return dict(feats=feats, adj_own=adj_own, adj_prev=adj_prev, adj_next=adj_next, bcount=bcount, wqkv=wqkv, w_mp=w_mp, w_out=w_out)


def reference(feats, adj_own, adj_prev, adj_next, bcount, wqkv, w_mp, w_out):
    rows = NODE_DEV
    feat_parts = feats.reshape(N_DOM, rows, D)
    zero_rim = jnp.zeros((1, BND, D), feats.dtype)
    prev_rim = jnp.concatenate([zero_rim, feat_parts[:-1, rows - BND:]], 0)
    next_rim = jnp.concatenate([feat_parts[1:, :BND], zero_rim], 0)
    part_ids = jnp.arange(N_DOM).astype(jnp.int32)[:, None]
    column = jnp.arange(BND).astype(jnp.int32)[None, :]
    prev_count = jnp.concatenate([jnp.zeros((1,), jnp.int32), bcount[:-1, 1]])
    next_count = jnp.concatenate([bcount[1:, 0], jnp.zeros((1,), jnp.int32)])
    prev_vis = (part_ids > 0) & (column >= BND - prev_count[:, None])
    next_vis = (part_ids < N_DOM - 1) & (column < next_count[:, None])
    own = adj_own.reshape(N_DOM, rows, rows).astype(jnp.float32)
    prv = jnp.where(prev_vis[:, None, :], adj_prev.reshape(N_DOM, rows, BND), 0).astype(jnp.float32)
    nxt = jnp.where(next_vis[:, None, :], adj_next.reshape(N_DOM, rows, BND), 0).astype(jnp.float32)
    degree = 1.0 + jnp.sum(own, -1) + jnp.sum(prv, -1) + jnp.sum(nxt, -1)
    total = feat_parts.astype(jnp.float32)
    total = total + jnp.einsum("prc,pcd->prd", own, feat_parts.astype(jnp.float32))
    total = total + jnp.einsum("prc,pcd->prd", prv, prev_rim.astype(jnp.float32))
    total = total + jnp.einsum("prc,pcd->prd", nxt, next_rim.astype(jnp.float32))
    mixed = (total / degree[..., None]).astype(jnp.bfloat16).reshape(NODES, D)
    local = jnp.dot(mixed, w_mp, preferred_element_type=jnp.float32)
    query = jnp.dot(feats, wqkv[0], preferred_element_type=jnp.float32).astype(jnp.bfloat16)
    key = jnp.dot(feats, wqkv[1], preferred_element_type=jnp.float32).astype(jnp.bfloat16)
    value = jnp.dot(feats, wqkv[2], preferred_element_type=jnp.float32).astype(jnp.bfloat16)
    head_size = D // HEADS
    scale = 1.0 / (head_size ** 0.5)

    def split_heads(array):
        return array.reshape(NODES, HEADS, head_size).transpose(1, 0, 2)

    def one_head(items):
        q_head, k_head, v_head = items
        score = jnp.dot(q_head, k_head.T, preferred_element_type=jnp.float32) * scale
        peak = jnp.max(score, -1, keepdims=True)
        expo = jnp.exp(score - peak)
        weight = (expo / jnp.sum(expo, -1, keepdims=True)).astype(jnp.bfloat16)
        return jnp.dot(weight, v_head, preferred_element_type=jnp.float32).astype(jnp.bfloat16)

    per_head = lax.map(one_head, (split_heads(query), split_heads(key), split_heads(value)))
    heads_out = per_head.transpose(1, 0, 2).reshape(NODES, D)
    attn = jnp.dot(heads_out, w_out, preferred_element_type=jnp.float32)
    return (feats.astype(jnp.float32) + local + attn).astype(jnp.bfloat16)
```

```python
import functools
import math

import jax
import jax.numpy as jnp
from jax import lax
from jax.experimental import pallas as pl
from jax.experimental.pallas import tpu as pltpu
from jax.sharding import PartitionSpec as P

HEADS = 32


def with_halo(cells, sides, width):
    for axis, dim in sides:
        count = lax.axis_size(axis)
        ends = count - 1
        head = lax.slice_in_dim(cells, 0, width, axis=dim)
        tail = lax.slice_in_dim(cells, cells.shape[dim] - width, cells.shape[dim], axis=dim)
        cells = jnp.concatenate(
            [
                lax.ppermute(tail, axis, [(i, (i + 1) % count) for i in range(ends)]),
                cells,
                lax.ppermute(head, axis, [((i + 1) % count, i) for i in range(ends)]),
            ],
            axis=dim,
        )
    return cells


def attend(head_qkv, head_size):
    nodes = head_qkv.shape[1]
    columns = head_qkv.shape[2]
    count_heads = columns // head_size
    query = head_qkv[0].reshape(nodes, count_heads, head_size)
    key = head_qkv[1].reshape(nodes, count_heads, head_size)
    value = head_qkv[2].reshape(nodes, count_heads, head_size)
    scale = 1.0 / head_size**0.5
    block = math.gcd(nodes, 512)

    def one_block(index):
        q_block = lax.dynamic_slice_in_dim(query, index * block, block, 0)
        score = jnp.einsum("qhc,khc->hqk", q_block, key, preferred_element_type=jnp.float32) * scale
        peak = jnp.max(score, -1, keepdims=True)
        expo = jnp.exp(score - peak)
        weight = (expo / jnp.sum(expo, -1, keepdims=True)).astype(jnp.bfloat16)
        result = jnp.einsum("hqk,khc->qhc", weight, value, preferred_element_type=jnp.float32)
        return result.astype(jnp.bfloat16).reshape(block, columns)

    blocks = lax.map(one_block, jnp.arange(nodes // block))
    return blocks.reshape(nodes, columns)


def message_term(mixed, w_mp):
    return jnp.dot(
        mixed, lax.all_gather(w_mp, "dom", axis=0, tiled=True), preferred_element_type=jnp.float32
    )


def body(feats, adj_own, adj_prev, adj_next, bcount, wqkv, w_mp, w_out):
    rows = feats.shape[0]
    width = feats.shape[1]
    band = adj_prev.shape[1]
    parts = lax.axis_size("dom")
    myself = lax.axis_index("dom")
    padded = with_halo(feats, (("dom", 0),), band)
    prev_rim = padded[:band]
    next_rim = padded[band + rows :]
    column = jnp.arange(band)
    prev_count = bcount[jnp.maximum(myself - 1, 0), 1]
    next_count = bcount[jnp.minimum(myself + 1, parts - 1), 0]
    prev_vis = (myself > 0) & (column >= band - prev_count)
    next_vis = (myself < parts - 1) & (column < next_count)
    own = adj_own.astype(jnp.bfloat16)
    prv = jnp.where(prev_vis[None, :], adj_prev, 0).astype(jnp.bfloat16)
    nxt = jnp.where(next_vis[None, :], adj_next, 0).astype(jnp.bfloat16)
    degree = (
        1.0
        + jnp.sum(own.astype(jnp.float32), -1)
        + jnp.sum(prv.astype(jnp.float32), -1)
        + jnp.sum(nxt.astype(jnp.float32), -1)
    )
    total = feats.astype(jnp.float32) + jnp.dot(own, feats, preferred_element_type=jnp.float32)
    total = total + jnp.dot(prv, prev_rim, preferred_element_type=jnp.float32)
    total = total + jnp.dot(nxt, next_rim, preferred_element_type=jnp.float32)
    mixed = (total / degree[:, None]).astype(jnp.bfloat16)
    node_qkv = jnp.einsum(
        "nd,tdc->tnc",
        feats,
        lax.all_gather(wqkv, "dom", axis=2, tiled=True),
        preferred_element_type=jnp.float32,
    ).astype(jnp.bfloat16)
    head_qkv = lax.all_to_all(node_qkv, "dom", split_axis=2, concat_axis=1, tiled=True)
    head_out = attend(head_qkv, width // HEADS)
    node_out = lax.all_to_all(head_out, "dom", split_axis=0, concat_axis=1, tiled=True)
    local = message_term(mixed, w_mp)
    attn = jnp.dot(
        node_out,
        lax.all_gather(w_out, "dom", axis=0, tiled=True),
        preferred_element_type=jnp.float32,
    )
    return (feats.astype(jnp.float32) + local + attn).astype(jnp.bfloat16)


def layer_kernel(
    head_size,
    feats, adj_own, adj_prev, adj_next, bcount, wqkv, w_mp, w_out, out,
    fall, own_adj, prev_adj, next_adj, counts, wcat, w2, qs, kt, v1, own_bits, rim_bits, rims, lhs,
    keep, rs_out, rs_in, relay_in,
    load_sem, sib_send, sib_recv, ag_send, ag_recv, adj_send, adj_recv, rs_send, rs_recv,
):
    rows, width = feats.shape
    cols = w_out.shape[0]
    band = adj_prev.shape[0]
    half = rows // 2
    heads = cols // head_size
    parts = counts.shape[1]
    me = lax.axis_index("dom")
    core = me % 2
    chip = me // 2
    sib = me + 1 - 2 * core
    cx, cy = chip % 2, chip // 2
    slot_chip = [cy * 2 + cx, cy * 2 + 1 - cx, (1 - cy) * 2 + cx, (1 - cy) * 2 + 1 - cx]
    x_dev, y_dev = slot_chip[1] * 2 + core, slot_chip[2] * 2 + core
    mesh_id = pl.DeviceIdType.MESH

    def remote(src, dst, send_sem, recv_sem, dev):
        return pltpu.make_async_remote_copy(
            src_ref=src, dst_ref=dst, send_sem=send_sem, recv_sem=recv_sem,
            device_id={"dom": dev}, device_id_type=mesh_id,
        )

    def col_at(k):
        return pl.ds(pl.multiple_of(k * cols, cols), cols)

    pairs = [(feats, fall.at[0])]
    pairs += [(wqkv.at[t], wcat.at[:, col_at(2 * t + core)]) for t in range(3)]
    pairs += [(adj_own, own_adj), (adj_prev, prev_adj), (adj_next, next_adj), (bcount, counts)]
    pairs += [(w_out, w2.at[col_at(core)]), (w_mp, w2.at[col_at(2 + core)])]
    loads = [pltpu.make_async_copy(a, b, load_sem.at[k]) for k, (a, b) in enumerate(pairs)]
    for load in loads:
        load.start()

    barrier = pltpu.get_barrier_semaphore()
    for dev in (x_dev, y_dev, sib):
        pl.semaphore_signal(barrier, inc=1, device_id={"dom": dev}, device_id_type=mesh_id)
    pl.semaphore_wait(barrier, 3)

    low, high = pl.ds(0, half), pl.ds(half, half)

    def gather(k, src, slot, span, dev):
        return remote(src, fall.at[slot, span], ag_send.at[k], ag_recv.at[k], dev)

    x_a = gather(0, feats.at[low], 1, low, x_dev)
    y_b = gather(1, feats.at[high], 2, high, y_dev)
    x_b = gather(2, feats.at[high], 1, high, x_dev)
    y_a = gather(3, feats.at[low], 2, low, y_dev)
    x_fwd = gather(4, fall.at[2, high], 3, high, x_dev)
    y_fwd = gather(5, fall.at[1, low], 3, low, y_dev)
    w_copies = [
        remote(wqkv.at[t], wcat.at[:, col_at(2 * t + core)], sib_send.at[t], sib_recv.at[t], sib)
        for t in range(3)
    ]
    w_copies += [
        remote(w_out, w2.at[col_at(core)], sib_send.at[3], sib_recv.at[3], sib),
        remote(w_mp, w2.at[col_at(2 + core)], sib_send.at[4], sib_recv.at[4], sib),
    ]
    chip_cols = pl.ds(pl.multiple_of(chip * 2 * cols, 2 * cols), 2 * cols)

    def rim_copies(s):
        return [
            remote(
                fall.at[s, pl.ds(e * (rows - band), band), chip_cols], rims.at[s, e],
                sib_send.at[5 + 2 * s + e], sib_recv.at[5 + 2 * s + e], sib,
            )
            for e in range(2)
        ]

    def kv_copies(k, s, n):
        own, theirs = pl.ds(s * rows, n * rows), pl.ds((4 + s) * rows, n * rows)
        lanes = pl.ds(0, cols)
        return [
            remote(kt.at[:, own], kt.at[:, theirs], sib_send.at[13 + 2 * k], sib_recv.at[13 + 2 * k], sib),
            remote(
                v1.at[:, own, lanes], v1.at[:, theirs, lanes],
                sib_send.at[14 + 2 * k], sib_recv.at[14 + 2 * k], sib,
            ),
        ]

    def adj(k, ref, src, dst, dev):
        return remote(ref.at[src], ref.at[dst], adj_send.at[k], adj_recv.at[k], dev)

    x_own, y_rim = adj(0, own_bits, 0, 1, x_dev), adj(1, rim_bits, 0, 2, y_dev)
    y_own_fwd, x_rim_fwd = adj(2, own_bits, 1, 3, y_dev), adj(3, rim_bits, 2, 3, x_dev)
    x_rim, y_own = adj(4, rim_bits, 0, 1, x_dev), adj(5, own_bits, 0, 2, y_dev)

    sent = []

    def start(*copies):
        for copy in copies:
            copy.start()
            sent.append(copy)

    start(x_a, y_b, *w_copies[:3], x_b, y_a, *w_copies[3:])

    v1[:, :, cols:] = jnp.ones_like(v1[:, :, cols:])
    lane_head = lax.broadcasted_iota(jnp.int32, (1, cols), 1) // head_size
    factor = math.log2(math.e) / head_size**0.5

    def project(s, n):
        block = fall[s] if n == 1 else fall[s : s + n].reshape(n * rows, width)
        r = jnp.dot(block, wcat[...], preferred_element_type=jnp.float32)
        for g in range(2):
            for i in range(n):
                q = r[i * rows : (i + 1) * rows, g * cols : (g + 1) * cols] * factor
                for h in range(heads):
                    qs[g, s + i, h * rows : (h + 1) * rows, :] = jnp.where(lane_head == h, q, 0.0).astype(
                        jnp.bfloat16
                    )
            v1[g, s * rows : (s + n) * rows, :cols] = r[:, (4 + g) * cols : (5 + g) * cols].astype(
                jnp.bfloat16
            )
        kt[:, s * rows : (s + n) * rows] = r[:, 2 * cols : 4 * cols].T.astype(jnp.bfloat16)

    for load in loads[4:8]:
        load.wait()
    before, after = (me + parts - 1) % parts, (me + 1) % parts
    column = lax.broadcasted_iota(jnp.int32, (band, 1), 0)
    device = lax.broadcasted_iota(jnp.int32, (1, parts), 1)
    prev_count = jnp.sum(jnp.where((device == before) & (me > 0), counts[1:2], 0), -1, keepdims=True)
    next_count = jnp.sum(
        jnp.where((device == after) & (me < parts - 1), counts[0:1], 0), -1, keepdims=True
    )
    own_bits[0] = own_adj[...].astype(jnp.float32).astype(jnp.bfloat16)
    rim_bits[0, :band] = (
        jnp.where(column >= band - prev_count, prev_adj[...], 0).astype(jnp.float32).astype(jnp.bfloat16)
    )
    rim_bits[0, band:] = (
        jnp.where(column < next_count, next_adj[...], 0).astype(jnp.float32).astype(jnp.bfloat16)
    )
    start(x_own, y_rim)

    for load in loads[:4]:
        load.wait()
    start(*rim_copies(0))
    for copy in w_copies[:3]:
        copy.wait_recv()
    project(0, 1)
    start(*kv_copies(0, 0, 1))

    x_a.wait_recv()
    start(y_fwd)
    y_b.wait_recv()
    start(x_fwd)
    x_b.wait_recv()
    y_a.wait_recv()
    x_own.wait_recv()
    start(y_own_fwd)
    y_rim.wait_recv()
    start(x_rim_fwd)
    start(x_rim, y_own)
    start(*rim_copies(1), *rim_copies(2))
    project(1, 2)
    start(*kv_copies(1, 1, 2))

    ones = jnp.ones((rows, cols), jnp.bfloat16)

    def mixing(s):
        def slot_of(c):
            c = (c + 4) % 4
            return (c % 2 + cx) % 2 + 2 * ((c // 2 + cy) % 2)

        prev_rim = rims[slot_of(slot_chip[s] - 1 + core), 1]
        next_rim = rims[slot_of(slot_chip[s] + core), 0]
        rim = jnp.concatenate([prev_rim, next_rim], 0)
        block = fall[s, :, chip_cols]
        own, pn = own_bits[s], rim_bits[s]
        contract = (((0,), (0,)), ((), ()))
        total = block.astype(jnp.float32)
        total += jnp.dot(own, block, preferred_element_type=jnp.float32)
        total += lax.dot_general(pn, rim, contract, preferred_element_type=jnp.float32)
        degree = 1.0 + jnp.dot(own, ones, preferred_element_type=jnp.float32)
        degree += lax.dot_general(pn, ones[: 2 * band], contract, preferred_element_type=jnp.float32)
        for g in range(2):
            lhs[:, (2 + g) * cols : (3 + g) * cols] = (
                total[:, g * cols : (g + 1) * cols] / degree
            ).astype(jnp.bfloat16)

    def attention(s):
        for g in range(2):
            top = jnp.zeros((rows, cols), jnp.float32)
            bottom = jnp.ones((rows, cols), jnp.float32)
            score = jnp.dot(
                qs[g, s], kt[g * cols : (g + 1) * cols, :], preferred_element_type=jnp.float32
            )
            peak = jnp.max(score, -1, keepdims=True)
            weight = jnp.exp2(score - peak).astype(jnp.bfloat16)
            both = jnp.dot(weight, v1[g], preferred_element_type=jnp.float32)
            for h in range(heads):
                mine = both[h * rows : (h + 1) * rows]
                top = jnp.where(lane_head == h, mine[:, :cols], top)
                bottom = jnp.where(lane_head == h, mine[:, cols:], bottom)
            lhs[:, g * cols : (g + 1) * cols] = (top / bottom).astype(jnp.bfloat16)

    def unit(s):
        mixing(s)
        attention(s)
        return jnp.dot(lhs[...], w2[...], preferred_element_type=jnp.float32)

    x_fwd.wait_recv()
    y_fwd.wait_recv()
    start(*rim_copies(3))
    project(3, 1)
    start(*kv_copies(2, 3, 1))

    y_own_fwd.wait_recv()
    x_rim_fwd.wait_recv()
    x_rim.wait_recv()
    y_own.wait_recv()
    for s in range(4):
        for copy in rim_copies(s):
            copy.wait_recv()
    for copy in kv_copies(0, 0, 1) + kv_copies(1, 1, 2) + kv_copies(2, 3, 1):
        copy.wait_recv()
    for load in loads[8:]:
        load.wait()
    for copy in w_copies[3:]:
        copy.wait_recv()

    x_relay = remote(rs_out.at[2, low], relay_in.at[0], rs_send.at[0], rs_recv.at[0], x_dev)
    y_relay = remote(rs_out.at[2, high], relay_in.at[1], rs_send.at[1], rs_recv.at[1], y_dev)
    x_low = remote(rs_out.at[0, low], rs_in.at[0, low], rs_send.at[2], rs_recv.at[2], x_dev)
    x_high = remote(rs_out.at[0, high], rs_in.at[0, high], rs_send.at[3], rs_recv.at[3], x_dev)
    y_low = remote(rs_out.at[1, low], rs_in.at[1, low], rs_send.at[4], rs_recv.at[4], y_dev)
    y_high = remote(rs_out.at[1, high], rs_in.at[1, high], rs_send.at[5], rs_recv.at[5], y_dev)

    rs_out[2] = unit(3).astype(jnp.bfloat16)
    start(x_relay, y_relay)
    part = unit(1)
    rs_out[0, low] = part[:half].astype(jnp.bfloat16)
    start(x_low)
    keep[0] = part[half:]
    part = unit(2)
    rs_out[1, high] = part[half:].astype(jnp.bfloat16)
    start(y_high)
    keep[1] = part[:half]
    y_relay.wait_recv()
    rs_out[0, high] = (keep[0] + relay_in[1].astype(jnp.float32)).astype(jnp.bfloat16)
    start(x_high)
    x_relay.wait_recv()
    rs_out[1, low] = (keep[1] + relay_in[0].astype(jnp.float32)).astype(jnp.bfloat16)
    start(y_low)
    part = unit(0) + fall[0].astype(jnp.float32)
    keep[2] = part[:half]
    keep[3] = part[half:]
    x_low.wait_recv()
    y_high.wait_recv()
    x_high.wait_recv()
    y_low.wait_recv()
    for k, span in enumerate((low, high)):
        out[span] = (
            keep[2 + k] + rs_in[0, span].astype(jnp.float32) + rs_in[1, span].astype(jnp.float32)
        ).astype(out.dtype)
    for copy in sent:
        copy.wait_send()


def fused_layer(feats, adj_own, adj_prev, adj_next, bcount, wqkv, w_mp, w_out):
    rows, width = feats.shape
    cols = w_out.shape[0]
    band = adj_prev.shape[1]
    nodes = rows * lax.axis_size("dom")
    head_size = width // HEADS
    heads = cols // head_size
    vmem = pl.BlockSpec(memory_space=pltpu.VMEM)
    hbm = pl.BlockSpec(memory_space=pltpu.HBM)
    bf16, f32 = jnp.bfloat16, jnp.float32
    dma = pltpu.SemaphoreType.DMA
    return pl.pallas_call(
        functools.partial(layer_kernel, head_size),
        out_shape=jax.ShapeDtypeStruct((rows, width), bf16),
        in_specs=[hbm] * 8,
        out_specs=vmem,
        scratch_shapes=[
            pltpu.VMEM((4, rows, width), bf16),
            pltpu.VMEM(adj_own.shape, adj_own.dtype),
            pltpu.VMEM(adj_prev.shape[::-1], adj_prev.dtype),
            pltpu.VMEM(adj_next.shape[::-1], adj_next.dtype),
            pltpu.VMEM(bcount.shape[::-1], bcount.dtype),
            pltpu.VMEM((width, 6 * cols), bf16),
            pltpu.VMEM((4 * cols, width), bf16),
            pltpu.VMEM((2, 4, heads * rows, cols), bf16),
            pltpu.VMEM((2 * cols, nodes), bf16),
            pltpu.VMEM((2, nodes, 2 * cols), bf16),
            pltpu.VMEM((4, rows, rows), bf16),
            pltpu.VMEM((4, 2 * band, rows), bf16),
            pltpu.VMEM((4, 2, band, 2 * cols), bf16),
            pltpu.VMEM((rows, 4 * cols), bf16),
            pltpu.VMEM((4, rows // 2, width), f32),
            pltpu.VMEM((3, rows, width), bf16),
            pltpu.VMEM((2, rows, width), bf16),
            pltpu.VMEM((2, rows // 2, width), bf16),
            dma((10,)),
            dma((19,)),
            dma((19,)),
            dma((6,)),
            dma((6,)),
            dma((6,)),
            dma((6,)),
            dma((6,)),
            dma((6,)),
        ],
        compiler_params=pltpu.CompilerParams(
            collective_id=0, has_side_effects=True, vmem_limit_bytes=64 * 1024 * 1024
        ),
    )(feats, adj_own, adj_prev.T, adj_next.T, bcount.T, wqkv, w_mp, w_out)


def solution(mesh):
    placed = (
        P(("dp", "dom"), None),
        P(("dp", "dom"), None),
        P(("dp", "dom"), None),
        P(("dp", "dom"), None),
        P("dp", None),
        P(None, None, "dom"),
        P("dom", None),
        P("dom", None),
    )
    layer = fused_layer if mesh.shape["dom"] == 8 else body
    return jax.shard_map(
        layer, mesh=mesh, in_specs=placed, out_specs=P(("dp", "dom"), None), check_vma=False
    )
```

```python
import functools
import math

import jax
import jax.numpy as jnp
from jax import lax
from jax.experimental import pallas as pl
from jax.experimental.pallas import tpu as pltpu
from jax.sharding import PartitionSpec as P

HEADS = 32


def with_halo(cells, sides, width):
    for axis, dim in sides:
        count = lax.axis_size(axis)
        ends = count - 1
        head = lax.slice_in_dim(cells, 0, width, axis=dim)
        tail = lax.slice_in_dim(cells, cells.shape[dim] - width, cells.shape[dim], axis=dim)
        cells = jnp.concatenate(
            [
                lax.ppermute(tail, axis, [(i, (i + 1) % count) for i in range(ends)]),
                cells,
                lax.ppermute(head, axis, [((i + 1) % count, i) for i in range(ends)]),
            ],
            axis=dim,
        )
    return cells


def attend(head_qkv, head_size):
    nodes = head_qkv.shape[1]
    columns = head_qkv.shape[2]
    count_heads = columns // head_size
    query = head_qkv[0].reshape(nodes, count_heads, head_size)
    key = head_qkv[1].reshape(nodes, count_heads, head_size)
    value = head_qkv[2].reshape(nodes, count_heads, head_size)
    scale = 1.0 / head_size**0.5
    block = math.gcd(nodes, 512)

    def one_block(index):
        q_block = lax.dynamic_slice_in_dim(query, index * block, block, 0)
        score = jnp.einsum("qhc,khc->hqk", q_block, key, preferred_element_type=jnp.float32) * scale
        peak = jnp.max(score, -1, keepdims=True)
        expo = jnp.exp(score - peak)
        weight = (expo / jnp.sum(expo, -1, keepdims=True)).astype(jnp.bfloat16)
        result = jnp.einsum("hqk,khc->qhc", weight, value, preferred_element_type=jnp.float32)
        return result.astype(jnp.bfloat16).reshape(block, columns)

    blocks = lax.map(one_block, jnp.arange(nodes // block))
    return blocks.reshape(nodes, columns)


def message_term(mixed, w_mp):
    return jnp.dot(
        mixed, lax.all_gather(w_mp, "dom", axis=0, tiled=True), preferred_element_type=jnp.float32
    )


def body(feats, adj_own, adj_prev, adj_next, bcount, wqkv, w_mp, w_out):
    rows = feats.shape[0]
    width = feats.shape[1]
    band = adj_prev.shape[1]
    parts = lax.axis_size("dom")
    myself = lax.axis_index("dom")
    padded = with_halo(feats, (("dom", 0),), band)
    prev_rim = padded[:band]
    next_rim = padded[band + rows :]
    column = jnp.arange(band)
    prev_count = bcount[jnp.maximum(myself - 1, 0), 1]
    next_count = bcount[jnp.minimum(myself + 1, parts - 1), 0]
    prev_vis = (myself > 0) & (column >= band - prev_count)
    next_vis = (myself < parts - 1) & (column < next_count)
    own = adj_own.astype(jnp.bfloat16)
    prv = jnp.where(prev_vis[None, :], adj_prev, 0).astype(jnp.bfloat16)
    nxt = jnp.where(next_vis[None, :], adj_next, 0).astype(jnp.bfloat16)
    degree = (
        1.0
        + jnp.sum(own.astype(jnp.float32), -1)
        + jnp.sum(prv.astype(jnp.float32), -1)
        + jnp.sum(nxt.astype(jnp.float32), -1)
    )
    total = feats.astype(jnp.float32) + jnp.dot(own, feats, preferred_element_type=jnp.float32)
    total = total + jnp.dot(prv, prev_rim, preferred_element_type=jnp.float32)
    total = total + jnp.dot(nxt, next_rim, preferred_element_type=jnp.float32)
    mixed = (total / degree[:, None]).astype(jnp.bfloat16)
    node_qkv = jnp.einsum(
        "nd,tdc->tnc",
        feats,
        lax.all_gather(wqkv, "dom", axis=2, tiled=True),
        preferred_element_type=jnp.float32,
    ).astype(jnp.bfloat16)
    head_qkv = lax.all_to_all(node_qkv, "dom", split_axis=2, concat_axis=1, tiled=True)
    head_out = attend(head_qkv, width // HEADS)
    node_out = lax.all_to_all(head_out, "dom", split_axis=0, concat_axis=1, tiled=True)
    local = message_term(mixed, w_mp)
    attn = jnp.dot(
        node_out,
        lax.all_gather(w_out, "dom", axis=0, tiled=True),
        preferred_element_type=jnp.float32,
    )
    return (feats.astype(jnp.float32) + local + attn).astype(jnp.bfloat16)


def layer_kernel(
    head_size,
    feats, adj_own, adj_prev, adj_next, bcount, wqkv, w_mp, w_out, out,
    fall, own_adj, prev_adj, next_adj, counts, wcat, w2, qs, kt, v1, own_bits, rim_bits, rims, lhs,
    keep, rs_out, rs_in, relay_in,
    load_sem, sib_send, sib_recv, ag_send, ag_recv, adj_send, adj_recv, rs_send, rs_recv,
):
    rows, width = feats.shape
    cols = w_out.shape[0]
    band = adj_prev.shape[0]
    half = rows // 2
    heads = cols // head_size
    parts = counts.shape[1]
    me = lax.axis_index("dom")
    core = me % 2
    chip = me // 2
    sib = me + 1 - 2 * core
    cx, cy = chip % 2, chip // 2
    slot_chip = [cy * 2 + cx, cy * 2 + 1 - cx, (1 - cy) * 2 + cx, (1 - cy) * 2 + 1 - cx]
    x_dev, y_dev = slot_chip[1] * 2 + core, slot_chip[2] * 2 + core
    mesh_id = pl.DeviceIdType.MESH

    def remote(src, dst, send_sem, recv_sem, dev):
        return pltpu.make_async_remote_copy(
            src_ref=src, dst_ref=dst, send_sem=send_sem, recv_sem=recv_sem,
            device_id={"dom": dev}, device_id_type=mesh_id,
        )

    def col_at(k):
        return pl.ds(pl.multiple_of(k * cols, cols), cols)

    pairs = [(feats, fall.at[0])]
    pairs += [(wqkv.at[t], wcat.at[:, col_at(2 * t + core)]) for t in range(3)]
    pairs += [(adj_own, own_adj), (adj_prev, prev_adj), (adj_next, next_adj), (bcount, counts)]
    pairs += [(w_out, w2.at[col_at(core)]), (w_mp, w2.at[col_at(2 + core)])]
    loads = [pltpu.make_async_copy(a, b, load_sem.at[k]) for k, (a, b) in enumerate(pairs)]
    for load in loads:
        load.start()

    barrier = pltpu.get_barrier_semaphore()
    for dev in (x_dev, y_dev, sib):
        pl.semaphore_signal(barrier, inc=1, device_id={"dom": dev}, device_id_type=mesh_id)
    pl.semaphore_wait(barrier, 3)

    low, high = pl.ds(0, half), pl.ds(half, half)

    def gather(k, src, slot, span, dev):
        return remote(src, fall.at[slot, span], ag_send.at[k], ag_recv.at[k], dev)

    x_a = gather(0, feats.at[low], 1, low, x_dev)
    y_b = gather(1, feats.at[high], 2, high, y_dev)
    x_b = gather(2, feats.at[high], 1, high, x_dev)
    y_a = gather(3, feats.at[low], 2, low, y_dev)
    x_fwd = gather(4, fall.at[2, high], 3, high, x_dev)
    y_fwd = gather(5, fall.at[1, low], 3, low, y_dev)
    w_copies = [
        remote(wqkv.at[t], wcat.at[:, col_at(2 * t + core)], sib_send.at[t], sib_recv.at[t], sib)
        for t in range(3)
    ]
    w_copies += [
        remote(w_out, w2.at[col_at(core)], sib_send.at[3], sib_recv.at[3], sib),
        remote(w_mp, w2.at[col_at(2 + core)], sib_send.at[4], sib_recv.at[4], sib),
    ]
    chip_cols = pl.ds(pl.multiple_of(chip * 2 * cols, 2 * cols), 2 * cols)

    def rim_copies(s):
        return [
            remote(
                fall.at[s, pl.ds(e * (rows - band), band), chip_cols], rims.at[s, e],
                sib_send.at[5 + 2 * s + e], sib_recv.at[5 + 2 * s + e], sib,
            )
            for e in range(2)
        ]

    def kv_copies(k, s, n):
        own, theirs = pl.ds(s * rows, n * rows), pl.ds((4 + s) * rows, n * rows)
        lanes = pl.ds(0, cols)
        return [
            remote(kt.at[:, own], kt.at[:, theirs], sib_send.at[13 + 2 * k], sib_recv.at[13 + 2 * k], sib),
            remote(
                v1.at[:, own, lanes], v1.at[:, theirs, lanes],
                sib_send.at[14 + 2 * k], sib_recv.at[14 + 2 * k], sib,
            ),
        ]

    def adj(k, ref, src, dst, dev):
        return remote(ref.at[src], ref.at[dst], adj_send.at[k], adj_recv.at[k], dev)

    x_own, y_rim = adj(0, own_bits, 0, 1, x_dev), adj(1, rim_bits, 0, 2, y_dev)
    y_own_fwd, x_rim_fwd = adj(2, own_bits, 1, 3, y_dev), adj(3, rim_bits, 2, 3, x_dev)
    x_rim, y_own = adj(4, rim_bits, 0, 1, x_dev), adj(5, own_bits, 0, 2, y_dev)

    sent = []

    def start(*copies):
        for copy in copies:
            copy.start()
            sent.append(copy)

    start(x_a, y_b, *w_copies[:3], x_b, y_a, *w_copies[3:])

    v1[:, :, cols:] = jnp.ones_like(v1[:, :, cols:])
    lane_head = lax.broadcasted_iota(jnp.int32, (1, cols), 1) // head_size
    factor = math.log2(math.e) / head_size**0.5

    def project(s, n):
        block = fall[s] if n == 1 else fall[s : s + n].reshape(n * rows, width)
        r = jnp.dot(block, wcat[...], preferred_element_type=jnp.float32)
        for g in range(2):
            for i in range(n):
                q = r[i * rows : (i + 1) * rows, g * cols : (g + 1) * cols] * factor
                for h in range(heads):
                    qs[g, s + i, h * rows : (h + 1) * rows, :] = jnp.where(lane_head == h, q, 0.0).astype(
                        jnp.bfloat16
                    )
            v1[g, s * rows : (s + n) * rows, :cols] = r[:, (4 + g) * cols : (5 + g) * cols].astype(
                jnp.bfloat16
            )
        kt[:, s * rows : (s + n) * rows] = r[:, 2 * cols : 4 * cols].T.astype(jnp.bfloat16)

    for load in loads[4:8]:
        load.wait()
    before, after = (me + parts - 1) % parts, (me + 1) % parts
    column = lax.broadcasted_iota(jnp.int32, (band, 1), 0)
    device = lax.broadcasted_iota(jnp.int32, (1, parts), 1)
    prev_count = jnp.sum(jnp.where((device == before) & (me > 0), counts[1:2], 0), -1, keepdims=True)
    next_count = jnp.sum(
        jnp.where((device == after) & (me < parts - 1), counts[0:1], 0), -1, keepdims=True
    )
    own_bits[0] = own_adj[...].astype(jnp.float32).astype(jnp.bfloat16)
    rim_bits[0, :band] = (
        jnp.where(column >= band - prev_count, prev_adj[...], 0).astype(jnp.float32).astype(jnp.bfloat16)
    )
    rim_bits[0, band:] = (
        jnp.where(column < next_count, next_adj[...], 0).astype(jnp.float32).astype(jnp.bfloat16)
    )
    start(x_own, y_rim)

    for load in loads[:4]:
        load.wait()
    start(*rim_copies(0))
    for copy in w_copies[:3]:
        copy.wait_recv()
    project(0, 1)
    start(*kv_copies(0, 0, 1))

    x_a.wait_recv()
    start(y_fwd)
    y_b.wait_recv()
    start(x_fwd)
    x_b.wait_recv()
    y_a.wait_recv()
    x_own.wait_recv()
    start(y_own_fwd)
    y_rim.wait_recv()
    start(x_rim_fwd)
    start(x_rim, y_own)
    start(*rim_copies(1), *rim_copies(2))
    project(1, 2)
    start(*kv_copies(1, 1, 2))

    ones = jnp.ones((rows, cols), jnp.bfloat16)

    def mixing(s):
        def slot_of(c):
            c = (c + 4) % 4
            return (c % 2 + cx) % 2 + 2 * ((c // 2 + cy) % 2)

        prev_rim = rims[slot_of(slot_chip[s] - 1 + core), 1]
        next_rim = rims[slot_of(slot_chip[s] + core), 0]
        rim = jnp.concatenate([prev_rim, next_rim], 0)
        block = fall[s, :, chip_cols]
        own, pn = own_bits[s], rim_bits[s]
        contract = (((0,), (0,)), ((), ()))
        total = block.astype(jnp.float32)
        total += jnp.dot(own, block, preferred_element_type=jnp.float32)
        total += lax.dot_general(pn, rim, contract, preferred_element_type=jnp.float32)
        degree = 1.0 + jnp.dot(own, ones, preferred_element_type=jnp.float32)
        degree += lax.dot_general(pn, ones[: 2 * band], contract, preferred_element_type=jnp.float32)
        for g in range(2):
            lhs[:, (2 + g) * cols : (3 + g) * cols] = (
                total[:, g * cols : (g + 1) * cols] / degree
            ).astype(jnp.bfloat16)

    def attention(s):
        for g in range(2):
            top = jnp.zeros((rows, cols), jnp.float32)
            bottom = jnp.ones((rows, cols), jnp.float32)
            score = jnp.dot(
                qs[g, s], kt[g * cols : (g + 1) * cols, :], preferred_element_type=jnp.float32
            )
            peak = jnp.max(score, -1, keepdims=True)
            weight = jnp.exp2(score - peak).astype(jnp.bfloat16)
            both = jnp.dot(weight, v1[g], preferred_element_type=jnp.float32)
            for h in range(heads):
                mine = both[h * rows : (h + 1) * rows]
                top = jnp.where(lane_head == h, mine[:, :cols], top)
                bottom = jnp.where(lane_head == h, mine[:, cols:], bottom)
            lhs[:, g * cols : (g + 1) * cols] = (top / bottom).astype(jnp.bfloat16)

    def unit(s):
        mixing(s)
        attention(s)
        return jnp.dot(lhs[...], w2[...], preferred_element_type=jnp.float32)

    x_fwd.wait_recv()
    y_fwd.wait_recv()
    start(*rim_copies(3))
    project(3, 1)
    start(*kv_copies(2, 3, 1))

    y_own_fwd.wait_recv()
    x_rim_fwd.wait_recv()
    x_rim.wait_recv()
    y_own.wait_recv()
    for s in range(4):
        for copy in rim_copies(s):
            copy.wait_recv()
    for copy in kv_copies(0, 0, 1) + kv_copies(1, 1, 2) + kv_copies(2, 3, 1):
        copy.wait_recv()
    for load in loads[8:]:
        load.wait()
    for copy in w_copies[3:]:
        copy.wait_recv()

    x_relay = remote(rs_out.at[2, low], relay_in.at[0], rs_send.at[0], rs_recv.at[0], x_dev)
    y_relay = remote(rs_out.at[2, high], relay_in.at[1], rs_send.at[1], rs_recv.at[1], y_dev)
    x_low = remote(rs_out.at[0, low], rs_in.at[0, low], rs_send.at[2], rs_recv.at[2], x_dev)
    x_high = remote(rs_out.at[0, high], rs_in.at[0, high], rs_send.at[3], rs_recv.at[3], x_dev)
    y_low = remote(rs_out.at[1, low], rs_in.at[1, low], rs_send.at[4], rs_recv.at[4], y_dev)
    y_high = remote(rs_out.at[1, high], rs_in.at[1, high], rs_send.at[5], rs_recv.at[5], y_dev)

    rs_out[2] = unit(3).astype(jnp.bfloat16)
    start(x_relay, y_relay)
    part = unit(1)
    rs_out[0, low] = part[:half].astype(jnp.bfloat16)
    start(x_low)
    keep[0] = part[half:]
    part = unit(2)
    rs_out[1, high] = part[half:].astype(jnp.bfloat16)
    start(y_high)
    keep[1] = part[:half]
    y_relay.wait_recv()
    rs_out[0, high] = (keep[0] + relay_in[1].astype(jnp.float32)).astype(jnp.bfloat16)
    start(x_high)
    x_relay.wait_recv()
    rs_out[1, low] = (keep[1] + relay_in[0].astype(jnp.float32)).astype(jnp.bfloat16)
    start(y_low)
    part = unit(0) + fall[0].astype(jnp.float32)
    keep[2] = part[:half]
    keep[3] = part[half:]
    x_low.wait_recv()
    y_high.wait_recv()
    x_high.wait_recv()
    y_low.wait_recv()
    for k, span in enumerate((low, high)):
        out[span] = (
            keep[2 + k] + rs_in[0, span].astype(jnp.float32) + rs_in[1, span].astype(jnp.float32)
        ).astype(out.dtype)
    for copy in sent:
        copy.wait_send()


def fused_layer(feats, adj_own, adj_prev, adj_next, bcount, wqkv, w_mp, w_out):
    rows, width = feats.shape
    cols = w_out.shape[0]
    band = adj_prev.shape[1]
    nodes = rows * lax.axis_size("dom")
    head_size = width // HEADS
    heads = cols // head_size
    vmem = pl.BlockSpec(memory_space=pltpu.VMEM)
    hbm = pl.BlockSpec(memory_space=pltpu.HBM)
    bf16, f32 = jnp.bfloat16, jnp.float32
    dma = pltpu.SemaphoreType.DMA
    operands = (feats, adj_own, adj_prev.T, adj_next.T, bcount.T, wqkv, w_mp, w_out)
    pinned = [pltpu.with_memory_space_constraint(a, pltpu.HBM) for a in operands]
    return pl.pallas_call(
        functools.partial(layer_kernel, head_size),
        out_shape=pltpu.VMEM((rows, width), bf16),
        in_specs=[hbm] * 8,
        out_specs=vmem,
        scratch_shapes=[
            pltpu.VMEM((4, rows, width), bf16),
            pltpu.VMEM(adj_own.shape, adj_own.dtype),
            pltpu.VMEM(adj_prev.shape[::-1], adj_prev.dtype),
            pltpu.VMEM(adj_next.shape[::-1], adj_next.dtype),
            pltpu.VMEM(bcount.shape[::-1], bcount.dtype),
            pltpu.VMEM((width, 6 * cols), bf16),
            pltpu.VMEM((4 * cols, width), bf16),
            pltpu.VMEM((2, 4, heads * rows, cols), bf16),
            pltpu.VMEM((2 * cols, nodes), bf16),
            pltpu.VMEM((2, nodes, 2 * cols), bf16),
            pltpu.VMEM((4, rows, rows), bf16),
            pltpu.VMEM((4, 2 * band, rows), bf16),
            pltpu.VMEM((4, 2, band, 2 * cols), bf16),
            pltpu.VMEM((rows, 4 * cols), bf16),
            pltpu.VMEM((4, rows // 2, width), f32),
            pltpu.VMEM((3, rows, width), bf16),
            pltpu.VMEM((2, rows, width), bf16),
            pltpu.VMEM((2, rows // 2, width), bf16),
            dma((10,)),
            dma((19,)),
            dma((19,)),
            dma((6,)),
            dma((6,)),
            dma((6,)),
            dma((6,)),
            dma((6,)),
            dma((6,)),
        ],
        compiler_params=pltpu.CompilerParams(
            collective_id=0, has_side_effects=True, vmem_limit_bytes=40 * 1024 * 1024
        ),
    )(*pinned)


def solution(mesh):
    placed = (
        P(("dp", "dom"), None),
        P(("dp", "dom"), None),
        P(("dp", "dom"), None),
        P(("dp", "dom"), None),
        P("dp", None),
        P(None, None, "dom"),
        P("dom", None),
        P("dom", None),
    )
    layer = fused_layer if mesh.shape["dom"] == 8 else body
    return jax.shard_map(
        layer, mesh=mesh, in_specs=placed, out_specs=P(("dp", "dom"), None), check_vma=False
    )
```

```python
import functools
import math

import jax
import jax.numpy as jnp
from jax import lax
from jax.experimental import pallas as pl
from jax.experimental.pallas import tpu as pltpu
from jax.sharding import PartitionSpec as P

HEADS = 32


def with_halo(cells, sides, width):
    for axis, dim in sides:
        count = lax.axis_size(axis)
        ends = count - 1
        head = lax.slice_in_dim(cells, 0, width, axis=dim)
        tail = lax.slice_in_dim(cells, cells.shape[dim] - width, cells.shape[dim], axis=dim)
        cells = jnp.concatenate(
            [
                lax.ppermute(tail, axis, [(i, (i + 1) % count) for i in range(ends)]),
                cells,
                lax.ppermute(head, axis, [((i + 1) % count, i) for i in range(ends)]),
            ],
            axis=dim,
        )
    return cells


def attend(head_qkv, head_size):
    nodes = head_qkv.shape[1]
    columns = head_qkv.shape[2]
    count_heads = columns // head_size
    query = head_qkv[0].reshape(nodes, count_heads, head_size)
    key = head_qkv[1].reshape(nodes, count_heads, head_size)
    value = head_qkv[2].reshape(nodes, count_heads, head_size)
    scale = 1.0 / head_size**0.5
    block = math.gcd(nodes, 512)

    def one_block(index):
        q_block = lax.dynamic_slice_in_dim(query, index * block, block, 0)
        score = jnp.einsum("qhc,khc->hqk", q_block, key, preferred_element_type=jnp.float32) * scale
        peak = jnp.max(score, -1, keepdims=True)
        expo = jnp.exp(score - peak)
        weight = (expo / jnp.sum(expo, -1, keepdims=True)).astype(jnp.bfloat16)
        result = jnp.einsum("hqk,khc->qhc", weight, value, preferred_element_type=jnp.float32)
        return result.astype(jnp.bfloat16).reshape(block, columns)

    blocks = lax.map(one_block, jnp.arange(nodes // block))
    return blocks.reshape(nodes, columns)


def message_term(mixed, w_mp):
    return jnp.dot(
        mixed, lax.all_gather(w_mp, "dom", axis=0, tiled=True), preferred_element_type=jnp.float32
    )


def body(feats, adj_own, adj_prev, adj_next, bcount, wqkv, w_mp, w_out):
    rows = feats.shape[0]
    width = feats.shape[1]
    band = adj_prev.shape[1]
    parts = lax.axis_size("dom")
    myself = lax.axis_index("dom")
    padded = with_halo(feats, (("dom", 0),), band)
    prev_rim = padded[:band]
    next_rim = padded[band + rows :]
    column = jnp.arange(band)
    prev_count = bcount[jnp.maximum(myself - 1, 0), 1]
    next_count = bcount[jnp.minimum(myself + 1, parts - 1), 0]
    prev_vis = (myself > 0) & (column >= band - prev_count)
    next_vis = (myself < parts - 1) & (column < next_count)
    own = adj_own.astype(jnp.bfloat16)
    prv = jnp.where(prev_vis[None, :], adj_prev, 0).astype(jnp.bfloat16)
    nxt = jnp.where(next_vis[None, :], adj_next, 0).astype(jnp.bfloat16)
    degree = (
        1.0
        + jnp.sum(own.astype(jnp.float32), -1)
        + jnp.sum(prv.astype(jnp.float32), -1)
        + jnp.sum(nxt.astype(jnp.float32), -1)
    )
    total = feats.astype(jnp.float32) + jnp.dot(own, feats, preferred_element_type=jnp.float32)
    total = total + jnp.dot(prv, prev_rim, preferred_element_type=jnp.float32)
    total = total + jnp.dot(nxt, next_rim, preferred_element_type=jnp.float32)
    mixed = (total / degree[:, None]).astype(jnp.bfloat16)
    node_qkv = jnp.einsum(
        "nd,tdc->tnc",
        feats,
        lax.all_gather(wqkv, "dom", axis=2, tiled=True),
        preferred_element_type=jnp.float32,
    ).astype(jnp.bfloat16)
    head_qkv = lax.all_to_all(node_qkv, "dom", split_axis=2, concat_axis=1, tiled=True)
    head_out = attend(head_qkv, width // HEADS)
    node_out = lax.all_to_all(head_out, "dom", split_axis=0, concat_axis=1, tiled=True)
    local = message_term(mixed, w_mp)
    attn = jnp.dot(
        node_out,
        lax.all_gather(w_out, "dom", axis=0, tiled=True),
        preferred_element_type=jnp.float32,
    )
    return (feats.astype(jnp.float32) + local + attn).astype(jnp.bfloat16)


def layer_kernel(
    head_size,
    feats, adj_own, adj_prev, adj_next, bcount, wqkv, w_mp, w_out, out,
    fall, own_adj, prev_adj, next_adj, counts, wcat, w2, qs, kt, v1, own_bits, rim_bits, rims, lhs,
    keep, rs_out, rs_in, relay_in,
    load_sem, sib_send, sib_recv, ag_send, ag_recv, adj_send, adj_recv, rs_send, rs_recv,
):
    rows, width = feats.shape
    cols = w_out.shape[0]
    band = adj_prev.shape[0]
    half = rows // 2
    heads = cols // head_size
    parts = counts.shape[1]
    me = lax.axis_index("dom")
    core = me % 2
    chip = me // 2
    sib = me + 1 - 2 * core
    cx, cy = chip % 2, chip // 2
    slot_chip = [cy * 2 + cx, cy * 2 + 1 - cx, (1 - cy) * 2 + cx, (1 - cy) * 2 + 1 - cx]
    x_dev, y_dev = slot_chip[1] * 2 + core, slot_chip[2] * 2 + core
    mesh_id = pl.DeviceIdType.MESH

    def remote(src, dst, send_sem, recv_sem, dev):
        return pltpu.make_async_remote_copy(
            src_ref=src, dst_ref=dst, send_sem=send_sem, recv_sem=recv_sem,
            device_id={"dom": dev}, device_id_type=mesh_id,
        )

    def col_at(k):
        return pl.ds(pl.multiple_of(k * cols, cols), cols)

    pairs = [(feats, fall.at[0])]
    pairs += [(wqkv.at[t], wcat.at[:, col_at(2 * t + core)]) for t in range(3)]
    pairs += [(adj_own, own_adj), (adj_prev, prev_adj), (adj_next, next_adj), (bcount, counts)]
    pairs += [(w_out, w2.at[col_at(core)]), (w_mp, w2.at[col_at(2 + core)])]
    loads = [pltpu.make_async_copy(a, b, load_sem.at[k]) for k, (a, b) in enumerate(pairs)]
    for load in loads:
        load.start()

    barrier = pltpu.get_barrier_semaphore()
    for dev in (x_dev, y_dev, sib):
        pl.semaphore_signal(barrier, inc=1, device_id={"dom": dev}, device_id_type=mesh_id)
    pl.semaphore_wait(barrier, 3)

    low, high = pl.ds(0, half), pl.ds(half, half)

    def gather(k, src, slot, span, dev):
        return remote(src, fall.at[slot, span], ag_send.at[k], ag_recv.at[k], dev)

    x_a = gather(0, feats.at[low], 1, low, x_dev)
    y_b = gather(1, feats.at[high], 2, high, y_dev)
    x_b = gather(2, feats.at[high], 1, high, x_dev)
    y_a = gather(3, feats.at[low], 2, low, y_dev)
    x_fwd = gather(4, fall.at[2, high], 3, high, x_dev)
    y_fwd = gather(5, fall.at[1, low], 3, low, y_dev)
    w_copies = [
        remote(wqkv.at[t], wcat.at[:, col_at(2 * t + core)], sib_send.at[t], sib_recv.at[t], sib)
        for t in range(3)
    ]
    w_copies += [
        remote(w_out, w2.at[col_at(core)], sib_send.at[3], sib_recv.at[3], sib),
        remote(w_mp, w2.at[col_at(2 + core)], sib_send.at[4], sib_recv.at[4], sib),
    ]
    chip_cols = pl.ds(pl.multiple_of(chip * 2 * cols, 2 * cols), 2 * cols)

    def rim_copies(s):
        return [
            remote(
                fall.at[s, pl.ds(e * (rows - band), band), chip_cols], rims.at[s, e],
                sib_send.at[5 + 2 * s + e], sib_recv.at[5 + 2 * s + e], sib,
            )
            for e in range(2)
        ]

    def key_at(s, theirs=False):
        return (6 * rows if s == 3 else s * rows) + theirs * (rows if s == 3 else 3 * rows)

    def kv_copies(k, s, n):
        own, theirs = pl.ds(key_at(s), n * rows), pl.ds(key_at(s, True), n * rows)
        lanes = pl.ds(0, cols)
        return [
            remote(kt.at[:, own], kt.at[:, theirs], sib_send.at[13 + 2 * k], sib_recv.at[13 + 2 * k], sib),
            remote(
                v1.at[:, own, lanes], v1.at[:, theirs, lanes],
                sib_send.at[14 + 2 * k], sib_recv.at[14 + 2 * k], sib,
            ),
        ]

    def adj(k, ref, src, dst, dev):
        return remote(ref.at[src], ref.at[dst], adj_send.at[k], adj_recv.at[k], dev)

    x_own, y_rim = adj(0, own_bits, 0, 1, x_dev), adj(1, rim_bits, 0, 2, y_dev)
    y_own_fwd, x_rim_fwd = adj(2, own_bits, 1, 3, y_dev), adj(3, rim_bits, 2, 3, x_dev)
    x_rim, y_own = adj(4, rim_bits, 0, 1, x_dev), adj(5, own_bits, 0, 2, y_dev)

    sent = []

    def start(*copies):
        for copy in copies:
            copy.start()
            sent.append(copy)

    start(x_a, y_b, *w_copies[:3], x_b, y_a, *w_copies[3:])

    v1[:, :, cols:] = jnp.ones_like(v1[:, :, cols:])
    lane_head = lax.broadcasted_iota(jnp.int32, (1, cols), 1) // head_size
    factor = math.log2(math.e) / head_size**0.5

    def project(s, n):
        block = fall[s] if n == 1 else fall[s : s + n].reshape(n * rows, width)
        r = jnp.dot(block, wcat[...], preferred_element_type=jnp.float32)
        for g in range(2):
            for i in range(n):
                q = r[i * rows : (i + 1) * rows, g * cols : (g + 1) * cols] * factor
                for h in range(heads):
                    qs[g, s + i, h * rows : (h + 1) * rows, :] = jnp.where(lane_head == h, q, 0.0).astype(
                        jnp.bfloat16
                    )
            v1[g, key_at(s) : key_at(s) + n * rows, :cols] = r[:, (4 + g) * cols : (5 + g) * cols].astype(
                jnp.bfloat16
            )
        kt[:, key_at(s) : key_at(s) + n * rows] = r[:, 2 * cols : 4 * cols].T.astype(jnp.bfloat16)

    for load in loads[4:8]:
        load.wait()
    before, after = (me + parts - 1) % parts, (me + 1) % parts
    column = lax.broadcasted_iota(jnp.int32, (band, 1), 0)
    device = lax.broadcasted_iota(jnp.int32, (1, parts), 1)
    prev_count = jnp.sum(jnp.where((device == before) & (me > 0), counts[1:2], 0), -1, keepdims=True)
    next_count = jnp.sum(
        jnp.where((device == after) & (me < parts - 1), counts[0:1], 0), -1, keepdims=True
    )
    own_bits[0] = own_adj[...].astype(jnp.float32).astype(jnp.bfloat16)
    rim_bits[0, :band] = (
        jnp.where(column >= band - prev_count, prev_adj[...], 0).astype(jnp.float32).astype(jnp.bfloat16)
    )
    rim_bits[0, band:] = (
        jnp.where(column < next_count, next_adj[...], 0).astype(jnp.float32).astype(jnp.bfloat16)
    )
    start(x_own, y_rim)

    for load in loads[:4]:
        load.wait()
    start(*rim_copies(0))
    for copy in w_copies[:3]:
        copy.wait_recv()
    project(0, 1)
    start(*kv_copies(0, 0, 1))

    x_a.wait_recv()
    start(y_fwd)
    y_b.wait_recv()
    start(x_fwd)
    x_b.wait_recv()
    y_a.wait_recv()
    project(1, 2)
    start(*kv_copies(1, 1, 2))
    x_own.wait_recv()
    start(y_own_fwd)
    y_rim.wait_recv()
    start(x_rim_fwd)
    start(*rim_copies(1), *rim_copies(2))

    ones = jnp.ones((rows, cols), jnp.bfloat16)

    def mixing(s):
        def slot_of(c):
            c = (c + 4) % 4
            return (c % 2 + cx) % 2 + 2 * ((c // 2 + cy) % 2)

        prev_rim = rims[slot_of(slot_chip[s] - 1 + core), 1]
        next_rim = rims[slot_of(slot_chip[s] + core), 0]
        rim = jnp.concatenate([prev_rim, next_rim], 0)
        block = fall[s, :, chip_cols]
        own, pn = own_bits[s], rim_bits[s]
        contract = (((0,), (0,)), ((), ()))
        total = block.astype(jnp.float32)
        total += jnp.dot(own, block, preferred_element_type=jnp.float32)
        total += lax.dot_general(pn, rim, contract, preferred_element_type=jnp.float32)
        degree = 1.0 + jnp.dot(own, ones, preferred_element_type=jnp.float32)
        degree += lax.dot_general(pn, ones[: 2 * band], contract, preferred_element_type=jnp.float32)
        for g in range(2):
            lhs[:, (2 + g) * cols : (3 + g) * cols] = (
                total[:, g * cols : (g + 1) * cols] / degree
            ).astype(jnp.bfloat16)

    def score_of(g, h, s, first, last):
        keys = kt[g * cols : (g + 1) * cols, first * rows : last * rows]
        query = qs[g, s, h * rows : (h + 1) * rows]
        return jnp.dot(query, keys, preferred_element_type=jnp.float32)

    def weigh(score, state):
        peak = jnp.max(score, -1, keepdims=True)
        if state is not None:
            peak = jnp.maximum(peak, state[0])
        return peak, jnp.exp2(score - peak).astype(jnp.bfloat16)

    def gathered(g, first, last, peak, weight, state):
        total = jnp.dot(weight, v1[g, first * rows : last * rows], preferred_element_type=jnp.float32)
        if state is not None:
            total += state[1] * jnp.exp2(state[0] - peak)
        return peak, total

    def pipeline(s, first, last, states):
        order = [(g, h) for g in range(2) for h in range(heads)]
        scores, weights = {}, {}
        for k in range(len(order) + 2):
            if k < len(order):
                scores[k] = score_of(*order[k], s, first, last)
            if 0 <= k - 1 < len(order):
                g, h = order[k - 1]
                weights[k - 1] = weigh(scores.pop(k - 1), None if states is None else states[g][h])
            if k >= 2:
                g, h = order[k - 2]
                yield g, h, gathered(g, first, last, *weights.pop(k - 2), None if states is None else states[g][h])

    def begin(s, last):
        states = [[None] * heads, [None] * heads]
        for g, h, state in pipeline(s, 0, last, None):
            states[g][h] = state
        return states

    def finish(s, first, states):
        if states[0] is None:
            states = None
        for g, h, (_, both) in pipeline(s, first, 8, states):
            if h == 0:
                top = jnp.zeros((rows, cols), jnp.float32)
                bottom = jnp.ones((rows, cols), jnp.float32)
            top = jnp.where(lane_head == h, both[:, :cols], top)
            bottom = jnp.where(lane_head == h, both[:, cols:], bottom)
            if h == heads - 1:
                lhs[:, g * cols : (g + 1) * cols] = (top / bottom).astype(jnp.bfloat16)

    def project_out():
        return jnp.dot(lhs[...], w2[...], preferred_element_type=jnp.float32)

    for copy in kv_copies(0, 0, 1):
        copy.wait_recv()
    begun_x = begin(1, 4)
    begun_y = begin(2, 4)

    x_fwd.wait_recv()
    y_fwd.wait_recv()
    start(*rim_copies(3))
    project(3, 1)
    start(*kv_copies(2, 3, 1))
    start(x_rim, y_own)
    for copy in kv_copies(1, 1, 2):
        copy.wait_recv()
    begun_d = begin(3, 7)

    y_own_fwd.wait_recv()
    x_rim_fwd.wait_recv()
    for s in range(4):
        for copy in rim_copies(s):
            copy.wait_recv()
    mixing(3)
    for load in loads[8:]:
        load.wait()
    for copy in w_copies[3:]:
        copy.wait_recv()
    for copy in kv_copies(2, 3, 1):
        copy.wait_recv()

    x_relay = remote(rs_out.at[2, low], relay_in.at[0], rs_send.at[0], rs_recv.at[0], x_dev)
    y_relay = remote(rs_out.at[2, high], relay_in.at[1], rs_send.at[1], rs_recv.at[1], y_dev)
    x_low = remote(rs_out.at[0, low], rs_in.at[0, low], rs_send.at[2], rs_recv.at[2], x_dev)
    x_high = remote(rs_out.at[0, high], rs_in.at[0, high], rs_send.at[3], rs_recv.at[3], x_dev)
    y_low = remote(rs_out.at[1, low], rs_in.at[1, low], rs_send.at[4], rs_recv.at[4], y_dev)
    y_high = remote(rs_out.at[1, high], rs_in.at[1, high], rs_send.at[5], rs_recv.at[5], y_dev)

    finish(3, 7, begun_d)
    rs_out[2] = project_out().astype(jnp.bfloat16)
    start(x_relay, y_relay)
    x_rim.wait_recv()
    y_own.wait_recv()
    mixing(2)
    finish(2, 4, begun_y)
    part = project_out()
    rs_out[1, high] = part[half:].astype(jnp.bfloat16)
    start(y_high)
    keep[1] = part[:half]
    mixing(1)
    finish(1, 4, begun_x)
    part = project_out()
    rs_out[0, low] = part[:half].astype(jnp.bfloat16)
    start(x_low)
    keep[0] = part[half:]
    mixing(0)
    finish(0, 0, [None, None])
    part = project_out() + fall[0].astype(jnp.float32)
    keep[2] = part[:half]
    keep[3] = part[half:]
    y_relay.wait_recv()
    rs_out[0, high] = (keep[0] + relay_in[1].astype(jnp.float32)).astype(jnp.bfloat16)
    start(x_high)
    x_relay.wait_recv()
    rs_out[1, low] = (keep[1] + relay_in[0].astype(jnp.float32)).astype(jnp.bfloat16)
    start(y_low)
    x_low.wait_recv()
    keep[2] += rs_in[0, low].astype(jnp.float32)
    y_high.wait_recv()
    keep[3] += rs_in[1, high].astype(jnp.float32)
    x_high.wait_recv()
    out[high] = (keep[3] + rs_in[0, high].astype(jnp.float32)).astype(out.dtype)
    y_low.wait_recv()
    out[low] = (keep[2] + rs_in[1, low].astype(jnp.float32)).astype(out.dtype)
    for copy in sent:
        copy.wait_send()


def fused_layer(feats, adj_own, adj_prev, adj_next, bcount, wqkv, w_mp, w_out):
    rows, width = feats.shape
    cols = w_out.shape[0]
    band = adj_prev.shape[1]
    nodes = rows * lax.axis_size("dom")
    head_size = width // HEADS
    heads = cols // head_size
    vmem = pl.BlockSpec(memory_space=pltpu.VMEM)
    hbm = pl.BlockSpec(memory_space=pltpu.HBM)
    bf16, f32 = jnp.bfloat16, jnp.float32
    dma = pltpu.SemaphoreType.DMA
    operands = (feats, adj_own, adj_prev.T, adj_next.T, bcount.T, wqkv, w_mp, w_out)
    pinned = [pltpu.with_memory_space_constraint(a, pltpu.HBM) for a in operands]
    return pl.pallas_call(
        functools.partial(layer_kernel, head_size),
        out_shape=pltpu.VMEM((rows, width), bf16),
        in_specs=[hbm] * 8,
        out_specs=vmem,
        scratch_shapes=[
            pltpu.VMEM((4, rows, width), bf16),
            pltpu.VMEM(adj_own.shape, adj_own.dtype),
            pltpu.VMEM(adj_prev.shape[::-1], adj_prev.dtype),
            pltpu.VMEM(adj_next.shape[::-1], adj_next.dtype),
            pltpu.VMEM(bcount.shape[::-1], bcount.dtype),
            pltpu.VMEM((width, 6 * cols), bf16),
            pltpu.VMEM((4 * cols, width), bf16),
            pltpu.VMEM((2, 4, heads * rows, cols), bf16),
            pltpu.VMEM((2 * cols, nodes), bf16),
            pltpu.VMEM((2, nodes, 2 * cols), bf16),
            pltpu.VMEM((4, rows, rows), bf16),
            pltpu.VMEM((4, 2 * band, rows), bf16),
            pltpu.VMEM((4, 2, band, 2 * cols), bf16),
            pltpu.VMEM((rows, 4 * cols), bf16),
            pltpu.VMEM((4, rows // 2, width), f32),
            pltpu.VMEM((3, rows, width), bf16),
            pltpu.VMEM((2, rows, width), bf16),
            pltpu.VMEM((2, rows // 2, width), bf16),
            dma((10,)),
            dma((19,)),
            dma((19,)),
            dma((6,)),
            dma((6,)),
            dma((6,)),
            dma((6,)),
            dma((6,)),
            dma((6,)),
        ],
        compiler_params=pltpu.CompilerParams(
            collective_id=0, has_side_effects=True, vmem_limit_bytes=40 * 1024 * 1024
        ),
    )(*pinned)


def solution(mesh):
    placed = (
        P(("dp", "dom"), None),
        P(("dp", "dom"), None),
        P(("dp", "dom"), None),
        P(("dp", "dom"), None),
        P("dp", None),
        P(None, None, "dom"),
        P("dom", None),
        P("dom", None),
    )
    layer = fused_layer if mesh.shape["dom"] == 8 else body
    return jax.shard_map(
        layer, mesh=mesh, in_specs=placed, out_specs=P(("dp", "dom"), None), check_vma=False
    )
```

```python
import functools
import math

import jax
import jax.numpy as jnp
from jax import lax
from jax.experimental import pallas as pl
from jax.experimental.pallas import tpu as pltpu
from jax.sharding import PartitionSpec as P

HEADS = 32


def with_halo(cells, sides, width):
    for axis, dim in sides:
        count = lax.axis_size(axis)
        ends = count - 1
        head = lax.slice_in_dim(cells, 0, width, axis=dim)
        tail = lax.slice_in_dim(cells, cells.shape[dim] - width, cells.shape[dim], axis=dim)
        cells = jnp.concatenate(
            [
                lax.ppermute(tail, axis, [(i, (i + 1) % count) for i in range(ends)]),
                cells,
                lax.ppermute(head, axis, [((i + 1) % count, i) for i in range(ends)]),
            ],
            axis=dim,
        )
    return cells


def attend(head_qkv, head_size):
    nodes = head_qkv.shape[1]
    columns = head_qkv.shape[2]
    count_heads = columns // head_size
    query = head_qkv[0].reshape(nodes, count_heads, head_size)
    key = head_qkv[1].reshape(nodes, count_heads, head_size)
    value = head_qkv[2].reshape(nodes, count_heads, head_size)
    scale = 1.0 / head_size**0.5
    block = math.gcd(nodes, 512)

    def one_block(index):
        q_block = lax.dynamic_slice_in_dim(query, index * block, block, 0)
        score = jnp.einsum("qhc,khc->hqk", q_block, key, preferred_element_type=jnp.float32) * scale
        peak = jnp.max(score, -1, keepdims=True)
        expo = jnp.exp(score - peak)
        weight = (expo / jnp.sum(expo, -1, keepdims=True)).astype(jnp.bfloat16)
        result = jnp.einsum("hqk,khc->qhc", weight, value, preferred_element_type=jnp.float32)
        return result.astype(jnp.bfloat16).reshape(block, columns)

    blocks = lax.map(one_block, jnp.arange(nodes // block))
    return blocks.reshape(nodes, columns)


def message_term(mixed, w_mp):
    return jnp.dot(
        mixed, lax.all_gather(w_mp, "dom", axis=0, tiled=True), preferred_element_type=jnp.float32
    )


def body(feats, adj_own, adj_prev, adj_next, bcount, wqkv, w_mp, w_out):
    rows = feats.shape[0]
    width = feats.shape[1]
    band = adj_prev.shape[1]
    parts = lax.axis_size("dom")
    myself = lax.axis_index("dom")
    padded = with_halo(feats, (("dom", 0),), band)
    prev_rim = padded[:band]
    next_rim = padded[band + rows :]
    column = jnp.arange(band)
    prev_count = bcount[jnp.maximum(myself - 1, 0), 1]
    next_count = bcount[jnp.minimum(myself + 1, parts - 1), 0]
    prev_vis = (myself > 0) & (column >= band - prev_count)
    next_vis = (myself < parts - 1) & (column < next_count)
    own = adj_own.astype(jnp.bfloat16)
    prv = jnp.where(prev_vis[None, :], adj_prev, 0).astype(jnp.bfloat16)
    nxt = jnp.where(next_vis[None, :], adj_next, 0).astype(jnp.bfloat16)
    degree = (
        1.0
        + jnp.sum(own.astype(jnp.float32), -1)
        + jnp.sum(prv.astype(jnp.float32), -1)
        + jnp.sum(nxt.astype(jnp.float32), -1)
    )
    total = feats.astype(jnp.float32) + jnp.dot(own, feats, preferred_element_type=jnp.float32)
    total = total + jnp.dot(prv, prev_rim, preferred_element_type=jnp.float32)
    total = total + jnp.dot(nxt, next_rim, preferred_element_type=jnp.float32)
    mixed = (total / degree[:, None]).astype(jnp.bfloat16)
    node_qkv = jnp.einsum(
        "nd,tdc->tnc",
        feats,
        lax.all_gather(wqkv, "dom", axis=2, tiled=True),
        preferred_element_type=jnp.float32,
    ).astype(jnp.bfloat16)
    head_qkv = lax.all_to_all(node_qkv, "dom", split_axis=2, concat_axis=1, tiled=True)
    head_out = attend(head_qkv, width // HEADS)
    node_out = lax.all_to_all(head_out, "dom", split_axis=0, concat_axis=1, tiled=True)
    local = message_term(mixed, w_mp)
    attn = jnp.dot(
        node_out,
        lax.all_gather(w_out, "dom", axis=0, tiled=True),
        preferred_element_type=jnp.float32,
    )
    return (feats.astype(jnp.float32) + local + attn).astype(jnp.bfloat16)


def layer_kernel(
    head_size,
    feats, adj_own, adj_prev, adj_next, bcount, wqkv, w_mp, w_out, out,
    fall, own_adj, prev_adj, next_adj, counts, wcat, w2, qs, kt, v1, adj_bits, rims, lhs,
    keep, rs_out, rs_in, relay_in,
    load_sem, sib_send, sib_recv, ag_send, ag_recv, adj_send, adj_recv, rs_send, rs_recv,
):
    rows, width = feats.shape
    cols = w_out.shape[0]
    band = adj_prev.shape[0]
    half = rows // 2
    heads = cols // head_size
    parts = counts.shape[1]
    me = lax.axis_index("dom")
    core = me % 2
    chip = me // 2
    sib = me + 1 - 2 * core
    cx, cy = chip % 2, chip // 2
    slot_chip = [cy * 2 + cx, cy * 2 + 1 - cx, (1 - cy) * 2 + cx, (1 - cy) * 2 + 1 - cx]
    x_dev, y_dev, d_dev = [slot_chip[k] * 2 + core for k in (1, 2, 3)]
    mesh_id = pl.DeviceIdType.MESH

    def remote(src, dst, send_sem, recv_sem, dev):
        return pltpu.make_async_remote_copy(
            src_ref=src, dst_ref=dst, send_sem=send_sem, recv_sem=recv_sem,
            device_id={"dom": dev}, device_id_type=mesh_id,
        )

    def col_at(k):
        return pl.ds(pl.multiple_of(k * cols, cols), cols)

    pairs = [(feats, fall.at[0])]
    pairs += [(wqkv.at[t], wcat.at[:, col_at(2 * t + core)]) for t in range(3)]
    pairs += [(adj_own, own_adj), (adj_prev, prev_adj), (adj_next, next_adj), (bcount, counts)]
    pairs += [(w_out, w2.at[col_at(core)]), (w_mp, w2.at[col_at(2 + core)])]
    loads = [pltpu.make_async_copy(a, b, load_sem.at[k]) for k, (a, b) in enumerate(pairs)]
    for load in loads:
        load.start()

    barrier = pltpu.get_barrier_semaphore()
    for dev in (x_dev, y_dev, sib):
        pl.semaphore_signal(barrier, inc=1, device_id={"dom": dev}, device_id_type=mesh_id)
    pl.semaphore_wait(barrier, 3)

    low, high = pl.ds(0, half), pl.ds(half, half)

    def gather(k, src, slot, span, dev):
        return remote(src, fall.at[slot, span], ag_send.at[k], ag_recv.at[k], dev)

    x_a = gather(0, feats.at[low], 1, low, x_dev)
    y_b = gather(1, feats.at[high], 2, high, y_dev)
    x_b = gather(2, feats.at[high], 1, high, x_dev)
    y_a = gather(3, feats.at[low], 2, low, y_dev)
    x_fwd = gather(4, fall.at[2, high], 3, high, x_dev)
    y_fwd = gather(5, fall.at[1, low], 3, low, y_dev)
    w_copies = [
        remote(wqkv.at[t], wcat.at[:, col_at(2 * t + core)], sib_send.at[t], sib_recv.at[t], sib)
        for t in range(3)
    ]
    w_copies += [
        remote(w_out, w2.at[col_at(core)], sib_send.at[3], sib_recv.at[3], sib),
        remote(w_mp, w2.at[col_at(2 + core)], sib_send.at[4], sib_recv.at[4], sib),
    ]
    chip_cols = pl.ds(pl.multiple_of(chip * 2 * cols, 2 * cols), 2 * cols)

    def rim_copies(s):
        return [
            remote(
                fall.at[s, pl.ds(e * (rows - band), band), chip_cols], rims.at[s, e],
                sib_send.at[5 + 2 * s + e], sib_recv.at[5 + 2 * s + e], sib,
            )
            for e in range(2)
        ]

    def key_at(s, theirs=False):
        return (6 * rows if s == 3 else s * rows) + theirs * (rows if s == 3 else 3 * rows)

    def kv_copies(k, s, n):
        own, theirs = pl.ds(key_at(s), n * rows), pl.ds(key_at(s, True), n * rows)
        lanes = pl.ds(0, cols)
        return [
            remote(kt.at[:, own], kt.at[:, theirs], sib_send.at[13 + 2 * k], sib_recv.at[13 + 2 * k], sib),
            remote(
                v1.at[:, own, lanes], v1.at[:, theirs, lanes],
                sib_send.at[14 + 2 * k], sib_recv.at[14 + 2 * k], sib,
            ),
        ]

    x_adj, y_adj, d_adj = [
        remote(adj_bits.at[0], adj_bits.at[k + 1], adj_send.at[k], adj_recv.at[k], dev)
        for k, dev in enumerate((x_dev, y_dev, d_dev))
    ]

    sent = []

    def start(*copies):
        for copy in copies:
            copy.start()
            sent.append(copy)

    start(x_a, y_b, *w_copies[:3], x_b, y_a, *w_copies[3:])

    v1[:, :, cols:] = jnp.ones_like(v1[:, :, cols:])
    lane_head = lax.broadcasted_iota(jnp.int32, (1, cols), 1) // head_size
    factor = math.log2(math.e) / head_size**0.5

    def project(s, n):
        block = fall[s] if n == 1 else fall[s : s + n].reshape(n * rows, width)
        r = jnp.dot(block, wcat[...], preferred_element_type=jnp.float32)
        for g in range(2):
            for i in range(n):
                q = r[i * rows : (i + 1) * rows, g * cols : (g + 1) * cols] * factor
                for h in range(heads):
                    qs[g, s + i, h * rows : (h + 1) * rows, :] = jnp.where(lane_head == h, q, 0.0).astype(
                        jnp.bfloat16
                    )
            v1[g, key_at(s) : key_at(s) + n * rows, :cols] = r[:, (4 + g) * cols : (5 + g) * cols].astype(
                jnp.bfloat16
            )
        kt[:, key_at(s) : key_at(s) + n * rows] = r[:, 2 * cols : 4 * cols].T.astype(jnp.bfloat16)

    for load in loads[4:8]:
        load.wait()
    before, after = (me + parts - 1) % parts, (me + 1) % parts
    column = lax.broadcasted_iota(jnp.int32, (band, 1), 0)
    device = lax.broadcasted_iota(jnp.int32, (1, parts), 1)
    prev_count = jnp.sum(jnp.where((device == before) & (me > 0), counts[1:2], 0), -1, keepdims=True)
    next_count = jnp.sum(
        jnp.where((device == after) & (me < parts - 1), counts[0:1], 0), -1, keepdims=True
    )
    adj_bits[0, :rows] = own_adj[...].astype(jnp.float32).astype(jnp.bfloat16)
    adj_bits[0, rows : rows + band] = (
        jnp.where(column >= band - prev_count, prev_adj[...], 0).astype(jnp.float32).astype(jnp.bfloat16)
    )
    adj_bits[0, rows + band :] = (
        jnp.where(column < next_count, next_adj[...], 0).astype(jnp.float32).astype(jnp.bfloat16)
    )

    for load in loads[:4]:
        load.wait()
    start(*rim_copies(0))
    for copy in w_copies[:3]:
        copy.wait_recv()
    project(0, 1)
    start(*kv_copies(0, 0, 1))

    x_a.wait_recv()
    start(y_fwd)
    y_b.wait_recv()
    start(x_fwd)
    x_b.wait_recv()
    y_a.wait_recv()
    project(1, 2)
    start(*kv_copies(1, 1, 2))
    start(d_adj)
    start(*rim_copies(1), *rim_copies(2))

    ones = jnp.ones((rows, cols), jnp.bfloat16)

    def mixing(s):
        def slot_of(c):
            c = (c + 4) % 4
            return (c % 2 + cx) % 2 + 2 * ((c // 2 + cy) % 2)

        prev_rim = rims[slot_of(slot_chip[s] - 1 + core), 1]
        next_rim = rims[slot_of(slot_chip[s] + core), 0]
        rim = jnp.concatenate([prev_rim, next_rim], 0)
        block = fall[s, :, chip_cols]
        own, pn = adj_bits[s, :rows], adj_bits[s, rows:]
        contract = (((0,), (0,)), ((), ()))
        total = block.astype(jnp.float32)
        total += jnp.dot(own, block, preferred_element_type=jnp.float32)
        total += lax.dot_general(pn, rim, contract, preferred_element_type=jnp.float32)
        degree = 1.0 + jnp.dot(own, ones, preferred_element_type=jnp.float32)
        degree += lax.dot_general(pn, ones[: 2 * band], contract, preferred_element_type=jnp.float32)
        for g in range(2):
            lhs[:, (2 + g) * cols : (3 + g) * cols] = (
                total[:, g * cols : (g + 1) * cols] / degree
            ).astype(jnp.bfloat16)

    def score_of(g, h, s, first, last):
        keys = kt[g * cols : (g + 1) * cols, first * rows : last * rows]
        query = qs[g, s, h * rows : (h + 1) * rows]
        return jnp.dot(query, keys, preferred_element_type=jnp.float32)

    def weigh(score, state):
        peak = jnp.max(score, -1, keepdims=True)
        if state is not None:
            peak = jnp.maximum(peak, state[0])
        return peak, jnp.exp2(score - peak).astype(jnp.bfloat16)

    def gathered(g, first, last, peak, weight, state):
        total = jnp.dot(weight, v1[g, first * rows : last * rows], preferred_element_type=jnp.float32)
        if state is not None:
            total += state[1] * jnp.exp2(state[0] - peak)
        return peak, total

    def pipeline(s, first, last, states):
        order = [(g, h) for g in range(2) for h in range(heads)]
        scores, weights = {}, {}
        for k in range(len(order) + 2):
            if k < len(order):
                scores[k] = score_of(*order[k], s, first, last)
            if 0 <= k - 1 < len(order):
                g, h = order[k - 1]
                weights[k - 1] = weigh(scores.pop(k - 1), None if states is None else states[g][h])
            if k >= 2:
                g, h = order[k - 2]
                yield g, h, gathered(g, first, last, *weights.pop(k - 2), None if states is None else states[g][h])

    def begin(s, last):
        states = [[None] * heads, [None] * heads]
        for g, h, state in pipeline(s, 0, last, None):
            states[g][h] = state
        return states

    def finish(s, first, states):
        if states[0] is None:
            states = None
        for g, h, (_, both) in pipeline(s, first, 8, states):
            if h == 0:
                top = jnp.zeros((rows, cols), jnp.float32)
                bottom = jnp.ones((rows, cols), jnp.float32)
            top = jnp.where(lane_head == h, both[:, :cols], top)
            bottom = jnp.where(lane_head == h, both[:, cols:], bottom)
            if h == heads - 1:
                lhs[:, g * cols : (g + 1) * cols] = (top / bottom).astype(jnp.bfloat16)

    def project_out():
        return jnp.dot(lhs[...], w2[...], preferred_element_type=jnp.float32)

    for copy in kv_copies(0, 0, 1):
        copy.wait_recv()
    begun_x = begin(1, 4)
    begun_y = begin(2, 4)

    x_fwd.wait_recv()
    y_fwd.wait_recv()
    start(*rim_copies(3))
    project(3, 1)
    start(*kv_copies(2, 3, 1))
    start(x_adj, y_adj)
    for copy in kv_copies(1, 1, 2):
        copy.wait_recv()
    begun_d = begin(3, 7)

    d_adj.wait_recv()
    for s in range(4):
        for copy in rim_copies(s):
            copy.wait_recv()
    mixing(3)
    for load in loads[8:]:
        load.wait()
    for copy in w_copies[3:]:
        copy.wait_recv()
    for copy in kv_copies(2, 3, 1):
        copy.wait_recv()

    x_relay = remote(rs_out.at[2, low], relay_in.at[0], rs_send.at[0], rs_recv.at[0], x_dev)
    y_relay = remote(rs_out.at[2, high], relay_in.at[1], rs_send.at[1], rs_recv.at[1], y_dev)
    x_low = remote(rs_out.at[0, low], rs_in.at[0, low], rs_send.at[2], rs_recv.at[2], x_dev)
    x_high = remote(rs_out.at[0, high], rs_in.at[0, high], rs_send.at[3], rs_recv.at[3], x_dev)
    y_low = remote(rs_out.at[1, low], rs_in.at[1, low], rs_send.at[4], rs_recv.at[4], y_dev)
    y_high = remote(rs_out.at[1, high], rs_in.at[1, high], rs_send.at[5], rs_recv.at[5], y_dev)

    finish(3, 7, begun_d)
    rs_out[2] = project_out().astype(jnp.bfloat16)
    start(x_relay, y_relay)
    y_adj.wait_recv()
    mixing(2)
    finish(2, 4, begun_y)
    part = project_out()
    rs_out[1, high] = part[half:].astype(jnp.bfloat16)
    start(y_high)
    keep[1] = part[:half]
    x_adj.wait_recv()
    mixing(1)
    finish(1, 4, begun_x)
    part = project_out()
    rs_out[0, low] = part[:half].astype(jnp.bfloat16)
    start(x_low)
    keep[0] = part[half:]
    mixing(0)
    finish(0, 0, [None, None])
    part = project_out() + fall[0].astype(jnp.float32)
    keep[2] = part[:half]
    keep[3] = part[half:]
    y_relay.wait_recv()
    rs_out[0, high] = (keep[0] + relay_in[1].astype(jnp.float32)).astype(jnp.bfloat16)
    start(x_high)
    x_relay.wait_recv()
    rs_out[1, low] = (keep[1] + relay_in[0].astype(jnp.float32)).astype(jnp.bfloat16)
    start(y_low)
    x_low.wait_recv()
    keep[2] += rs_in[0, low].astype(jnp.float32)
    y_high.wait_recv()
    keep[3] += rs_in[1, high].astype(jnp.float32)
    x_high.wait_recv()
    out[high] = (keep[3] + rs_in[0, high].astype(jnp.float32)).astype(out.dtype)
    y_low.wait_recv()
    out[low] = (keep[2] + rs_in[1, low].astype(jnp.float32)).astype(out.dtype)
    for copy in sent:
        copy.wait_send()


def fused_layer(feats, adj_own, adj_prev, adj_next, bcount, wqkv, w_mp, w_out):
    rows, width = feats.shape
    cols = w_out.shape[0]
    band = adj_prev.shape[1]
    nodes = rows * lax.axis_size("dom")
    head_size = width // HEADS
    heads = cols // head_size
    vmem = pl.BlockSpec(memory_space=pltpu.VMEM)
    hbm = pl.BlockSpec(memory_space=pltpu.HBM)
    bf16, f32 = jnp.bfloat16, jnp.float32
    dma = pltpu.SemaphoreType.DMA
    operands = (feats, adj_own, adj_prev.T, adj_next.T, bcount.T, wqkv, w_mp, w_out)
    pinned = [pltpu.with_memory_space_constraint(a, pltpu.HBM) for a in operands]
    return pl.pallas_call(
        functools.partial(layer_kernel, head_size),
        out_shape=pltpu.VMEM((rows, width), bf16),
        in_specs=[hbm] * 8,
        out_specs=vmem,
        scratch_shapes=[
            pltpu.VMEM((4, rows, width), bf16),
            pltpu.VMEM(adj_own.shape, adj_own.dtype),
            pltpu.VMEM(adj_prev.shape[::-1], adj_prev.dtype),
            pltpu.VMEM(adj_next.shape[::-1], adj_next.dtype),
            pltpu.VMEM(bcount.shape[::-1], bcount.dtype),
            pltpu.VMEM((width, 6 * cols), bf16),
            pltpu.VMEM((4 * cols, width), bf16),
            pltpu.VMEM((2, 4, heads * rows, cols), bf16),
            pltpu.VMEM((2 * cols, nodes), bf16),
            pltpu.VMEM((2, nodes, 2 * cols), bf16),
            pltpu.VMEM((4, rows + 2 * band, rows), bf16),
            pltpu.VMEM((4, 2, band, 2 * cols), bf16),
            pltpu.VMEM((rows, 4 * cols), bf16),
            pltpu.VMEM((4, rows // 2, width), f32),
            pltpu.VMEM((3, rows, width), bf16),
            pltpu.VMEM((2, rows, width), bf16),
            pltpu.VMEM((2, rows // 2, width), bf16),
            dma((10,)),
            dma((19,)),
            dma((19,)),
            dma((6,)),
            dma((6,)),
            dma((3,)),
            dma((3,)),
            dma((6,)),
            dma((6,)),
        ],
        compiler_params=pltpu.CompilerParams(
            collective_id=0, has_side_effects=True, vmem_limit_bytes=40 * 1024 * 1024
        ),
    )(*pinned)


def solution(mesh):
    placed = (
        P(("dp", "dom"), None),
        P(("dp", "dom"), None),
        P(("dp", "dom"), None),
        P(("dp", "dom"), None),
        P("dp", None),
        P(None, None, "dom"),
        P("dom", None),
        P("dom", None),
    )
    layer = fused_layer if mesh.shape["dom"] == 8 else body
    return jax.shard_map(
        layer, mesh=mesh, in_specs=placed, out_specs=P(("dp", "dom"), None), check_vma=False
    )
```

```python
import functools
import math

import jax
import jax.numpy as jnp
from jax import lax
from jax.experimental import pallas as pl
from jax.experimental.pallas import tpu as pltpu
from jax.sharding import PartitionSpec as P

HEADS = 32


def with_halo(cells, sides, width):
    for axis, dim in sides:
        count = lax.axis_size(axis)
        ends = count - 1
        head = lax.slice_in_dim(cells, 0, width, axis=dim)
        tail = lax.slice_in_dim(cells, cells.shape[dim] - width, cells.shape[dim], axis=dim)
        cells = jnp.concatenate(
            [
                lax.ppermute(tail, axis, [(i, (i + 1) % count) for i in range(ends)]),
                cells,
                lax.ppermute(head, axis, [((i + 1) % count, i) for i in range(ends)]),
            ],
            axis=dim,
        )
    return cells


def attend(head_qkv, head_size):
    nodes = head_qkv.shape[1]
    columns = head_qkv.shape[2]
    count_heads = columns // head_size
    query = head_qkv[0].reshape(nodes, count_heads, head_size)
    key = head_qkv[1].reshape(nodes, count_heads, head_size)
    value = head_qkv[2].reshape(nodes, count_heads, head_size)
    scale = 1.0 / head_size**0.5
    block = math.gcd(nodes, 512)

    def one_block(index):
        q_block = lax.dynamic_slice_in_dim(query, index * block, block, 0)
        score = jnp.einsum("qhc,khc->hqk", q_block, key, preferred_element_type=jnp.float32) * scale
        peak = jnp.max(score, -1, keepdims=True)
        expo = jnp.exp(score - peak)
        weight = (expo / jnp.sum(expo, -1, keepdims=True)).astype(jnp.bfloat16)
        result = jnp.einsum("hqk,khc->qhc", weight, value, preferred_element_type=jnp.float32)
        return result.astype(jnp.bfloat16).reshape(block, columns)

    blocks = lax.map(one_block, jnp.arange(nodes // block))
    return blocks.reshape(nodes, columns)


def message_term(mixed, w_mp):
    return jnp.dot(
        mixed, lax.all_gather(w_mp, "dom", axis=0, tiled=True), preferred_element_type=jnp.float32
    )


def body(feats, adj_own, adj_prev, adj_next, bcount, wqkv, w_mp, w_out):
    rows = feats.shape[0]
    width = feats.shape[1]
    band = adj_prev.shape[1]
    parts = lax.axis_size("dom")
    myself = lax.axis_index("dom")
    padded = with_halo(feats, (("dom", 0),), band)
    prev_rim = padded[:band]
    next_rim = padded[band + rows :]
    column = jnp.arange(band)
    prev_count = bcount[jnp.maximum(myself - 1, 0), 1]
    next_count = bcount[jnp.minimum(myself + 1, parts - 1), 0]
    prev_vis = (myself > 0) & (column >= band - prev_count)
    next_vis = (myself < parts - 1) & (column < next_count)
    own = adj_own.astype(jnp.bfloat16)
    prv = jnp.where(prev_vis[None, :], adj_prev, 0).astype(jnp.bfloat16)
    nxt = jnp.where(next_vis[None, :], adj_next, 0).astype(jnp.bfloat16)
    degree = (
        1.0
        + jnp.sum(own.astype(jnp.float32), -1)
        + jnp.sum(prv.astype(jnp.float32), -1)
        + jnp.sum(nxt.astype(jnp.float32), -1)
    )
    total = feats.astype(jnp.float32) + jnp.dot(own, feats, preferred_element_type=jnp.float32)
    total = total + jnp.dot(prv, prev_rim, preferred_element_type=jnp.float32)
    total = total + jnp.dot(nxt, next_rim, preferred_element_type=jnp.float32)
    mixed = (total / degree[:, None]).astype(jnp.bfloat16)
    node_qkv = jnp.einsum(
        "nd,tdc->tnc",
        feats,
        lax.all_gather(wqkv, "dom", axis=2, tiled=True),
        preferred_element_type=jnp.float32,
    ).astype(jnp.bfloat16)
    head_qkv = lax.all_to_all(node_qkv, "dom", split_axis=2, concat_axis=1, tiled=True)
    head_out = attend(head_qkv, width // HEADS)
    node_out = lax.all_to_all(head_out, "dom", split_axis=0, concat_axis=1, tiled=True)
    local = message_term(mixed, w_mp)
    attn = jnp.dot(
        node_out,
        lax.all_gather(w_out, "dom", axis=0, tiled=True),
        preferred_element_type=jnp.float32,
    )
    return (feats.astype(jnp.float32) + local + attn).astype(jnp.bfloat16)


def layer_kernel(
    head_size,
    feats, adj_own, adj_prev, adj_next, bcount, wqkv, w_mp, w_out, out,
    fall, own_adj, prev_adj, next_adj, counts, wcat, w2, qs, kt, v1, adj_bits, rims, lhs,
    keep, rs_out, rs_in, relay_in,
    load_sem, sib_send, sib_recv, ag_send, ag_recv, adj_send, adj_recv, rs_send, rs_recv,
):
    rows, width = feats.shape
    cols = w_out.shape[0]
    band = adj_prev.shape[0]
    half = rows // 2
    heads = cols // head_size
    parts = counts.shape[1]
    me = lax.axis_index("dom")
    core = me % 2
    chip = me // 2
    sib = me + 1 - 2 * core
    cx, cy = chip % 2, chip // 2
    slot_chip = [cy * 2 + cx, cy * 2 + 1 - cx, (1 - cy) * 2 + cx, (1 - cy) * 2 + 1 - cx]
    x_dev, y_dev, d_dev = [slot_chip[k] * 2 + core for k in (1, 2, 3)]
    mesh_id = pl.DeviceIdType.MESH

    def remote(src, dst, send_sem, recv_sem, dev):
        return pltpu.make_async_remote_copy(
            src_ref=src, dst_ref=dst, send_sem=send_sem, recv_sem=recv_sem,
            device_id={"dom": dev}, device_id_type=mesh_id,
        )

    def col_at(k):
        return pl.ds(pl.multiple_of(k * cols, cols), cols)

    pairs = [(feats, fall.at[0])]
    pairs += [(wqkv.at[t], wcat.at[:, col_at(2 * t + core)]) for t in range(3)]
    pairs += [(adj_own, own_adj), (adj_prev, prev_adj), (adj_next, next_adj), (bcount, counts)]
    pairs += [(w_out, w2.at[col_at(core)]), (w_mp, w2.at[col_at(2 + core)])]
    loads = [pltpu.make_async_copy(a, b, load_sem.at[k]) for k, (a, b) in enumerate(pairs)]
    for load in loads:
        load.start()

    barrier = pltpu.get_barrier_semaphore()
    for dev in (x_dev, y_dev, sib):
        pl.semaphore_signal(barrier, inc=1, device_id={"dom": dev}, device_id_type=mesh_id)
    pl.semaphore_wait(barrier, 3)

    low, high = pl.ds(0, half), pl.ds(half, half)

    def gather(k, src, slot, span, dev):
        return remote(src, fall.at[slot, span], ag_send.at[k], ag_recv.at[k], dev)

    x_a = gather(0, feats.at[low], 1, low, x_dev)
    y_b = gather(1, feats.at[high], 2, high, y_dev)
    x_b = gather(2, feats.at[high], 1, high, x_dev)
    y_a = gather(3, feats.at[low], 2, low, y_dev)
    x_fwd = gather(4, fall.at[2, high], 3, high, x_dev)
    y_fwd = gather(5, fall.at[1, low], 3, low, y_dev)
    w_copies = [
        remote(wqkv.at[t], wcat.at[:, col_at(2 * t + core)], sib_send.at[t], sib_recv.at[t], sib)
        for t in range(3)
    ]
    w_copies += [
        remote(w_out, w2.at[col_at(core)], sib_send.at[3], sib_recv.at[3], sib),
        remote(w_mp, w2.at[col_at(2 + core)], sib_send.at[4], sib_recv.at[4], sib),
    ]
    chip_cols = pl.ds(pl.multiple_of(chip * 2 * cols, 2 * cols), 2 * cols)

    def rim_copies(s):
        return [
            remote(
                fall.at[s, pl.ds(e * (rows - band), band), chip_cols], rims.at[s, e],
                sib_send.at[5 + 2 * s + e], sib_recv.at[5 + 2 * s + e], sib,
            )
            for e in range(2)
        ]

    def key_at(s, theirs=False):
        return (6 * rows if s == 3 else s * rows) + theirs * (rows if s == 3 else 3 * rows)

    def kv_copies(k, s, n):
        own, theirs = pl.ds(key_at(s), n * rows), pl.ds(key_at(s, True), n * rows)
        lanes = pl.ds(0, cols)
        return [
            remote(kt.at[:, own], kt.at[:, theirs], sib_send.at[13 + 2 * k], sib_recv.at[13 + 2 * k], sib),
            remote(
                v1.at[:, own, lanes], v1.at[:, theirs, lanes],
                sib_send.at[14 + 2 * k], sib_recv.at[14 + 2 * k], sib,
            ),
        ]

    x_adj, y_adj, d_adj = [
        remote(adj_bits.at[0], adj_bits.at[k + 1], adj_send.at[k], adj_recv.at[k], dev)
        for k, dev in enumerate((x_dev, y_dev, d_dev))
    ]

    sent = []

    def start(*copies):
        for copy in copies:
            copy.start()
            sent.append(copy)

    start(x_a, y_b, *w_copies[:3], x_b, y_a, *w_copies[3:])

    v1[:, :, cols:] = jnp.ones_like(v1[:, :, cols:])
    lane_head = lax.broadcasted_iota(jnp.int32, (1, cols), 1) // head_size
    factor = math.log2(math.e) / head_size**0.5

    def project_kv(s, n):
        block = fall[s : s + n].reshape(n * rows, width)
        r = jnp.dot(block, wcat[:, 2 * cols :], preferred_element_type=jnp.float32)
        span = slice(key_at(s), key_at(s) + n * rows)
        for g in range(2):
            v1[g, span, :cols] = r[:, (2 + g) * cols : (3 + g) * cols].astype(jnp.bfloat16)
        kt[:, span] = r[:, : 2 * cols].T.astype(jnp.bfloat16)

    def project_q(s, n):
        block = fall[s : s + n].reshape(n * rows, width)
        r = jnp.dot(block, wcat[:, : 2 * cols], preferred_element_type=jnp.float32)
        for i in range(n):
            for g in range(2):
                q = r[i * rows : (i + 1) * rows, g * cols : (g + 1) * cols] * factor
                for h in range(heads):
                    qs[g, s + i, h * rows : (h + 1) * rows, :] = jnp.where(lane_head == h, q, 0.0).astype(
                        jnp.bfloat16
                    )

    for load in loads[4:8]:
        load.wait()
    before, after = (me + parts - 1) % parts, (me + 1) % parts
    column = lax.broadcasted_iota(jnp.int32, (band, 1), 0)
    device = lax.broadcasted_iota(jnp.int32, (1, parts), 1)
    prev_count = jnp.sum(jnp.where((device == before) & (me > 0), counts[1:2], 0), -1, keepdims=True)
    next_count = jnp.sum(
        jnp.where((device == after) & (me < parts - 1), counts[0:1], 0), -1, keepdims=True
    )
    adj_bits[0, :rows] = own_adj[...].astype(jnp.float32).astype(jnp.bfloat16)
    adj_bits[0, rows : rows + band] = (
        jnp.where(column >= band - prev_count, prev_adj[...], 0).astype(jnp.float32).astype(jnp.bfloat16)
    )
    adj_bits[0, rows + band :] = (
        jnp.where(column < next_count, next_adj[...], 0).astype(jnp.float32).astype(jnp.bfloat16)
    )

    for load in loads[:4]:
        load.wait()
    start(*rim_copies(0))
    for copy in w_copies[:3]:
        copy.wait_recv()
    project_kv(0, 1)
    start(*kv_copies(0, 0, 1))
    project_q(0, 1)

    x_a.wait_recv()
    start(y_fwd)
    y_b.wait_recv()
    start(x_fwd)
    x_b.wait_recv()
    y_a.wait_recv()
    project_kv(1, 2)
    start(*kv_copies(1, 1, 2))
    start(d_adj)
    project_q(1, 2)
    start(*rim_copies(1), *rim_copies(2))

    ones = jnp.ones((rows, cols), jnp.bfloat16)

    def mixing(s):
        def slot_of(c):
            c = (c + 4) % 4
            return (c % 2 + cx) % 2 + 2 * ((c // 2 + cy) % 2)

        prev_rim = rims[slot_of(slot_chip[s] - 1 + core), 1]
        next_rim = rims[slot_of(slot_chip[s] + core), 0]
        rim = jnp.concatenate([prev_rim, next_rim], 0)
        block = fall[s, :, chip_cols]
        own, pn = adj_bits[s, :rows], adj_bits[s, rows:]
        contract = (((0,), (0,)), ((), ()))
        total = block.astype(jnp.float32)
        total += jnp.dot(own, block, preferred_element_type=jnp.float32)
        total += lax.dot_general(pn, rim, contract, preferred_element_type=jnp.float32)
        degree = 1.0 + jnp.dot(own, ones, preferred_element_type=jnp.float32)
        degree += lax.dot_general(pn, ones[: 2 * band], contract, preferred_element_type=jnp.float32)
        for g in range(2):
            lhs[:, (2 + g) * cols : (3 + g) * cols] = (
                total[:, g * cols : (g + 1) * cols] / degree
            ).astype(jnp.bfloat16)

    def score_of(s, g, h, n, first, last):
        keys = kt[g * cols : (g + 1) * cols, first * rows : last * rows]
        query = qs[g, s, h * rows : (h + n) * rows]
        return jnp.dot(query, keys, preferred_element_type=jnp.float32)

    def weigh(score, state):
        peak = jnp.max(score, -1, keepdims=True)
        if state is not None:
            peak = jnp.maximum(peak, state[0])
        return peak, jnp.exp2(score - peak).astype(jnp.bfloat16)

    def gathered(g, first, last, peak, weight, state):
        total = jnp.dot(weight, v1[g, first * rows : last * rows], preferred_element_type=jnp.float32)
        if state is not None:
            total += state[1] * jnp.exp2(state[0] - peak)
        return peak, total

    def pipeline(s, first, last, states, n):
        order = [(g, h) for g in range(2) for h in range(0, heads, n)]
        scores, weights = {}, {}

        def state(g, h):
            if states is None:
                return None
            return [jnp.concatenate([states[g, h + k][e] for k in range(n)], 0) for e in range(2)]

        for k in range(len(order) + 2):
            if k < len(order):
                scores[k] = score_of(s, *order[k], n, first, last)
            if 0 <= k - 1 < len(order):
                weights[k - 1] = weigh(scores.pop(k - 1), state(*order[k - 1]))
            if k >= 2:
                g, h = order[k - 2]
                peak, total = gathered(g, first, last, *weights.pop(k - 2), state(g, h))
                for e in range(n):
                    span = slice(e * rows, (e + 1) * rows)
                    yield (g, h + e), (peak[span], total[span])

    def begin(s, last):
        return dict(pipeline(s, 0, last, None, 1))

    def finish(s, first, states, n):
        for (g, h), (_, both) in pipeline(s, first, 8, states, n):
            if h == 0:
                top = jnp.zeros((rows, cols), jnp.float32)
                bottom = jnp.ones((rows, cols), jnp.float32)
            top = jnp.where(lane_head == h, both[:, :cols], top)
            bottom = jnp.where(lane_head == h, both[:, cols:], bottom)
            if h == heads - 1:
                lhs[:, g * cols : (g + 1) * cols] = (top / bottom).astype(jnp.bfloat16)

    def project_out():
        return jnp.dot(lhs[...], w2[...], preferred_element_type=jnp.float32)

    for copy in kv_copies(0, 0, 1):
        copy.wait_recv()
    begun_x = begin(1, 4)
    begun_y = begin(2, 4)

    x_fwd.wait_recv()
    y_fwd.wait_recv()
    start(*rim_copies(3))
    start(x_adj, y_adj)
    project_kv(3, 1)
    start(*kv_copies(2, 3, 1))
    for copy in kv_copies(1, 1, 2):
        copy.wait_recv()
    project_q(3, 1)
    begun_d = begin(3, 6)

    d_adj.wait_recv()
    for s in range(4):
        for copy in rim_copies(s):
            copy.wait_recv()
    mixing(3)
    for load in loads[8:]:
        load.wait()
    for copy in w_copies[3:]:
        copy.wait_recv()

    x_relay = remote(rs_out.at[2, low], relay_in.at[0], rs_send.at[0], rs_recv.at[0], x_dev)
    y_relay = remote(rs_out.at[2, high], relay_in.at[1], rs_send.at[1], rs_recv.at[1], y_dev)
    x_low = remote(rs_out.at[0, low], rs_in.at[0, low], rs_send.at[2], rs_recv.at[2], x_dev)
    x_high = remote(rs_out.at[0, high], rs_in.at[0, high], rs_send.at[3], rs_recv.at[3], x_dev)
    y_low = remote(rs_out.at[1, low], rs_in.at[1, low], rs_send.at[4], rs_recv.at[4], y_dev)
    y_high = remote(rs_out.at[1, high], rs_in.at[1, high], rs_send.at[5], rs_recv.at[5], y_dev)

    local = jnp.dot(lhs[:, 2 * cols :], w2[2 * cols :], preferred_element_type=jnp.float32)
    for copy in kv_copies(2, 3, 1):
        copy.wait_recv()
    finish(3, 6, begun_d, 1)
    attn = jnp.dot(lhs[:, : 2 * cols], w2[: 2 * cols], preferred_element_type=jnp.float32)
    rs_out[2] = (local + attn).astype(jnp.bfloat16)
    start(x_relay, y_relay)
    finish(2, 4, begun_y, 1)
    y_adj.wait_recv()
    mixing(2)
    part = project_out()
    rs_out[1, high] = part[half:].astype(jnp.bfloat16)
    start(y_high)
    keep[1] = part[:half]
    finish(1, 4, begun_x, 1)
    x_adj.wait_recv()
    mixing(1)
    part = project_out()
    rs_out[0, low] = part[:half].astype(jnp.bfloat16)
    start(x_low)
    keep[0] = part[half:]
    mixing(0)
    finish(0, 0, None, 1)
    part = project_out() + fall[0].astype(jnp.float32)
    keep[2] = part[:half]
    keep[3] = part[half:]
    y_relay.wait_recv()
    rs_out[0, high] = (keep[0] + relay_in[1].astype(jnp.float32)).astype(jnp.bfloat16)
    start(x_high)
    x_relay.wait_recv()
    rs_out[1, low] = (keep[1] + relay_in[0].astype(jnp.float32)).astype(jnp.bfloat16)
    start(y_low)
    x_low.wait_recv()
    keep[2] += rs_in[0, low].astype(jnp.float32)
    y_high.wait_recv()
    keep[3] += rs_in[1, high].astype(jnp.float32)
    x_high.wait_recv()
    out[high] = (keep[3] + rs_in[0, high].astype(jnp.float32)).astype(out.dtype)
    y_low.wait_recv()
    out[low] = (keep[2] + rs_in[1, low].astype(jnp.float32)).astype(out.dtype)
    for copy in sent:
        copy.wait_send()


def fused_layer(feats, adj_own, adj_prev, adj_next, bcount, wqkv, w_mp, w_out):
    rows, width = feats.shape
    cols = w_out.shape[0]
    band = adj_prev.shape[1]
    nodes = rows * lax.axis_size("dom")
    head_size = width // HEADS
    heads = cols // head_size
    vmem = pl.BlockSpec(memory_space=pltpu.VMEM)
    hbm = pl.BlockSpec(memory_space=pltpu.HBM)
    bf16, f32 = jnp.bfloat16, jnp.float32
    dma = pltpu.SemaphoreType.DMA
    operands = (feats, adj_own, adj_prev.T, adj_next.T, bcount.T, wqkv, w_mp, w_out)
    pinned = [pltpu.with_memory_space_constraint(a, pltpu.HBM) for a in operands]
    return pl.pallas_call(
        functools.partial(layer_kernel, head_size),
        out_shape=pltpu.VMEM((rows, width), bf16),
        in_specs=[hbm] * 8,
        out_specs=vmem,
        scratch_shapes=[
            pltpu.VMEM((4, rows, width), bf16),
            pltpu.VMEM(adj_own.shape, adj_own.dtype),
            pltpu.VMEM(adj_prev.shape[::-1], adj_prev.dtype),
            pltpu.VMEM(adj_next.shape[::-1], adj_next.dtype),
            pltpu.VMEM(bcount.shape[::-1], bcount.dtype),
            pltpu.VMEM((width, 6 * cols), bf16),
            pltpu.VMEM((4 * cols, width), bf16),
            pltpu.VMEM((2, 4, heads * rows, cols), bf16),
            pltpu.VMEM((2 * cols, nodes), bf16),
            pltpu.VMEM((2, nodes, 2 * cols), bf16),
            pltpu.VMEM((4, rows + 2 * band, rows), bf16),
            pltpu.VMEM((4, 2, band, 2 * cols), bf16),
            pltpu.VMEM((rows, 4 * cols), bf16),
            pltpu.VMEM((4, rows // 2, width), f32),
            pltpu.VMEM((3, rows, width), bf16),
            pltpu.VMEM((2, rows, width), bf16),
            pltpu.VMEM((2, rows // 2, width), bf16),
            dma((10,)),
            dma((19,)),
            dma((19,)),
            dma((6,)),
            dma((6,)),
            dma((3,)),
            dma((3,)),
            dma((6,)),
            dma((6,)),
        ],
        compiler_params=pltpu.CompilerParams(
            collective_id=0, has_side_effects=True, vmem_limit_bytes=40 * 1024 * 1024
        ),
    )(*pinned)


def solution(mesh):
    placed = (
        P(("dp", "dom"), None),
        P(("dp", "dom"), None),
        P(("dp", "dom"), None),
        P(("dp", "dom"), None),
        P("dp", None),
        P(None, None, "dom"),
        P("dom", None),
        P("dom", None),
    )
    layer = fused_layer if mesh.shape["dom"] == 8 else body
    return jax.shard_map(
        layer, mesh=mesh, in_specs=placed, out_specs=P(("dp", "dom"), None), check_vma=False
    )
```

```python
import functools
import math

import jax
import jax.numpy as jnp
from jax import lax
from jax.experimental import pallas as pl
from jax.experimental.pallas import tpu as pltpu
from jax.sharding import PartitionSpec as P

HEADS = 32


def with_halo(cells, sides, width):
    for axis, dim in sides:
        count = lax.axis_size(axis)
        ends = count - 1
        head = lax.slice_in_dim(cells, 0, width, axis=dim)
        tail = lax.slice_in_dim(cells, cells.shape[dim] - width, cells.shape[dim], axis=dim)
        cells = jnp.concatenate(
            [
                lax.ppermute(tail, axis, [(i, (i + 1) % count) for i in range(ends)]),
                cells,
                lax.ppermute(head, axis, [((i + 1) % count, i) for i in range(ends)]),
            ],
            axis=dim,
        )
    return cells


def attend(head_qkv, head_size):
    nodes = head_qkv.shape[1]
    columns = head_qkv.shape[2]
    count_heads = columns // head_size
    query = head_qkv[0].reshape(nodes, count_heads, head_size)
    key = head_qkv[1].reshape(nodes, count_heads, head_size)
    value = head_qkv[2].reshape(nodes, count_heads, head_size)
    scale = 1.0 / head_size**0.5
    block = math.gcd(nodes, 512)

    def one_block(index):
        q_block = lax.dynamic_slice_in_dim(query, index * block, block, 0)
        score = jnp.einsum("qhc,khc->hqk", q_block, key, preferred_element_type=jnp.float32) * scale
        peak = jnp.max(score, -1, keepdims=True)
        expo = jnp.exp(score - peak)
        weight = (expo / jnp.sum(expo, -1, keepdims=True)).astype(jnp.bfloat16)
        result = jnp.einsum("hqk,khc->qhc", weight, value, preferred_element_type=jnp.float32)
        return result.astype(jnp.bfloat16).reshape(block, columns)

    blocks = lax.map(one_block, jnp.arange(nodes // block))
    return blocks.reshape(nodes, columns)


def message_term(mixed, w_mp):
    return jnp.dot(
        mixed, lax.all_gather(w_mp, "dom", axis=0, tiled=True), preferred_element_type=jnp.float32
    )


def body(feats, adj_own, adj_prev, adj_next, bcount, wqkv, w_mp, w_out):
    rows = feats.shape[0]
    width = feats.shape[1]
    band = adj_prev.shape[1]
    parts = lax.axis_size("dom")
    myself = lax.axis_index("dom")
    padded = with_halo(feats, (("dom", 0),), band)
    prev_rim = padded[:band]
    next_rim = padded[band + rows :]
    column = jnp.arange(band)
    prev_count = bcount[jnp.maximum(myself - 1, 0), 1]
    next_count = bcount[jnp.minimum(myself + 1, parts - 1), 0]
    prev_vis = (myself > 0) & (column >= band - prev_count)
    next_vis = (myself < parts - 1) & (column < next_count)
    own = adj_own.astype(jnp.bfloat16)
    prv = jnp.where(prev_vis[None, :], adj_prev, 0).astype(jnp.bfloat16)
    nxt = jnp.where(next_vis[None, :], adj_next, 0).astype(jnp.bfloat16)
    degree = (
        1.0
        + jnp.sum(own.astype(jnp.float32), -1)
        + jnp.sum(prv.astype(jnp.float32), -1)
        + jnp.sum(nxt.astype(jnp.float32), -1)
    )
    total = feats.astype(jnp.float32) + jnp.dot(own, feats, preferred_element_type=jnp.float32)
    total = total + jnp.dot(prv, prev_rim, preferred_element_type=jnp.float32)
    total = total + jnp.dot(nxt, next_rim, preferred_element_type=jnp.float32)
    mixed = (total / degree[:, None]).astype(jnp.bfloat16)
    node_qkv = jnp.einsum(
        "nd,tdc->tnc",
        feats,
        lax.all_gather(wqkv, "dom", axis=2, tiled=True),
        preferred_element_type=jnp.float32,
    ).astype(jnp.bfloat16)
    head_qkv = lax.all_to_all(node_qkv, "dom", split_axis=2, concat_axis=1, tiled=True)
    head_out = attend(head_qkv, width // HEADS)
    node_out = lax.all_to_all(head_out, "dom", split_axis=0, concat_axis=1, tiled=True)
    local = message_term(mixed, w_mp)
    attn = jnp.dot(
        node_out,
        lax.all_gather(w_out, "dom", axis=0, tiled=True),
        preferred_element_type=jnp.float32,
    )
    return (feats.astype(jnp.float32) + local + attn).astype(jnp.bfloat16)


def layer_kernel(
    head_size,
    feats, adj_own, adj_prev, adj_next, bcount, wqkv, w_mp, w_out, out,
    fall, own_adj, prev_adj, next_adj, counts, wcat, w2, qs, kt, v1, adj_bits, rims, lhs,
    keep, rs_out, rs_in, relay_in,
    load_sem, sib_send, sib_recv, ag_send, ag_recv, adj_send, adj_recv, rs_send, rs_recv,
):
    rows, width = feats.shape
    cols = w_out.shape[0]
    band = adj_prev.shape[0]
    half = rows // 2
    heads = cols // head_size
    parts = counts.shape[1]
    me = lax.axis_index("dom")
    core = me % 2
    chip = me // 2
    sib = me + 1 - 2 * core
    cx, cy = chip % 2, chip // 2
    slot_chip = [cy * 2 + cx, cy * 2 + 1 - cx, (1 - cy) * 2 + cx, (1 - cy) * 2 + 1 - cx]
    x_dev, y_dev, d_dev = [slot_chip[k] * 2 + core for k in (1, 2, 3)]
    mesh_id = pl.DeviceIdType.MESH

    def remote(src, dst, send_sem, recv_sem, dev):
        return pltpu.make_async_remote_copy(
            src_ref=src, dst_ref=dst, send_sem=send_sem, recv_sem=recv_sem,
            device_id={"dom": dev}, device_id_type=mesh_id,
        )

    def col_at(k):
        return pl.ds(pl.multiple_of(k * cols, cols), cols)

    pairs = [(feats, fall.at[0])]
    pairs += [(wqkv.at[t], wcat.at[:, col_at(2 * t + core)]) for t in range(3)]
    pairs += [(adj_own, own_adj), (adj_prev, prev_adj), (adj_next, next_adj), (bcount, counts)]
    pairs += [(w_out, w2.at[col_at(core)]), (w_mp, w2.at[col_at(2 + core)])]
    loads = [pltpu.make_async_copy(a, b, load_sem.at[k]) for k, (a, b) in enumerate(pairs)]
    for load in loads:
        load.start()

    barrier = pltpu.get_barrier_semaphore()
    for dev in (x_dev, y_dev, sib):
        pl.semaphore_signal(barrier, inc=1, device_id={"dom": dev}, device_id_type=mesh_id)
    pl.semaphore_wait(barrier, 3)

    low, high = pl.ds(0, half), pl.ds(half, half)

    def gather(k, src, slot, span, dev):
        return remote(src, fall.at[slot, span], ag_send.at[k], ag_recv.at[k], dev)

    x_a = gather(0, feats.at[low], 1, low, x_dev)
    y_b = gather(1, feats.at[high], 2, high, y_dev)
    x_b = gather(2, feats.at[high], 1, high, x_dev)
    y_a = gather(3, feats.at[low], 2, low, y_dev)
    x_fwd = gather(4, fall.at[2, high], 3, high, x_dev)
    y_fwd = gather(5, fall.at[1, low], 3, low, y_dev)
    w_copies = [
        remote(wqkv.at[t], wcat.at[:, col_at(2 * t + core)], sib_send.at[t], sib_recv.at[t], sib)
        for t in range(3)
    ]
    w_copies += [
        remote(w_out, w2.at[col_at(core)], sib_send.at[3], sib_recv.at[3], sib),
        remote(w_mp, w2.at[col_at(2 + core)], sib_send.at[4], sib_recv.at[4], sib),
    ]
    chip_cols = pl.ds(pl.multiple_of(chip * 2 * cols, 2 * cols), 2 * cols)

    def rim_copies(s):
        return [
            remote(
                fall.at[s, pl.ds(e * (rows - band), band), chip_cols], rims.at[s, e],
                sib_send.at[5 + 2 * s + e], sib_recv.at[5 + 2 * s + e], sib,
            )
            for e in range(2)
        ]

    def key_at(s, theirs=False):
        return (6 * rows if s == 3 else s * rows) + theirs * (rows if s == 3 else 3 * rows)

    def kv_copies(k, s, n):
        own, theirs = pl.ds(key_at(s), n * rows), pl.ds(key_at(s, True), n * rows)
        lanes = pl.ds(0, cols)
        return [
            remote(kt.at[:, own], kt.at[:, theirs], sib_send.at[13 + 2 * k], sib_recv.at[13 + 2 * k], sib),
            remote(
                v1.at[:, own, lanes], v1.at[:, theirs, lanes],
                sib_send.at[14 + 2 * k], sib_recv.at[14 + 2 * k], sib,
            ),
        ]

    x_adj, y_adj, d_adj = [
        remote(adj_bits.at[0], adj_bits.at[k + 1], adj_send.at[k], adj_recv.at[k], dev)
        for k, dev in enumerate((x_dev, y_dev, d_dev))
    ]

    sent = []

    def start(*copies):
        for copy in copies:
            copy.start()
            sent.append(copy)

    start(x_a, y_b, *w_copies[:3], x_b, y_a, *w_copies[3:])

    v1[:, :, cols:] = jnp.ones_like(v1[:, :, cols:])
    lane_head = lax.broadcasted_iota(jnp.int32, (1, cols), 1) // head_size
    factor = math.log2(math.e) / head_size**0.5

    def project_kv(s, n):
        block = fall[s : s + n].reshape(n * rows, width)
        r = jnp.dot(block, wcat[:, 2 * cols :], preferred_element_type=jnp.float32)
        span = slice(key_at(s), key_at(s) + n * rows)
        for g in range(2):
            v1[g, span, :cols] = r[:, (2 + g) * cols : (3 + g) * cols].astype(jnp.bfloat16)
        kt[:, span] = r[:, : 2 * cols].T.astype(jnp.bfloat16)

    def project_q(s, n):
        block = fall[s : s + n].reshape(n * rows, width)
        r = jnp.dot(block, wcat[:, : 2 * cols], preferred_element_type=jnp.float32)
        for i in range(n):
            for g in range(2):
                q = r[i * rows : (i + 1) * rows, g * cols : (g + 1) * cols] * factor
                for h in range(heads):
                    qs[g, s + i, h * rows : (h + 1) * rows, :] = jnp.where(lane_head == h, q, 0.0).astype(
                        jnp.bfloat16
                    )

    for load in loads[4:8]:
        load.wait()
    before, after = (me + parts - 1) % parts, (me + 1) % parts
    column = lax.broadcasted_iota(jnp.int32, (band, 1), 0)
    device = lax.broadcasted_iota(jnp.int32, (1, parts), 1)
    prev_count = jnp.sum(jnp.where((device == before) & (me > 0), counts[1:2], 0), -1, keepdims=True)
    next_count = jnp.sum(
        jnp.where((device == after) & (me < parts - 1), counts[0:1], 0), -1, keepdims=True
    )
    adj_bits[0, :rows] = own_adj[...].astype(jnp.float32).astype(jnp.bfloat16)
    adj_bits[0, rows : rows + band] = (
        jnp.where(column >= band - prev_count, prev_adj[...], 0).astype(jnp.float32).astype(jnp.bfloat16)
    )
    adj_bits[0, rows + band :] = (
        jnp.where(column < next_count, next_adj[...], 0).astype(jnp.float32).astype(jnp.bfloat16)
    )

    for load in loads[:4]:
        load.wait()
    start(*rim_copies(0))
    for copy in w_copies[:3]:
        copy.wait_recv()
    project_kv(0, 1)
    start(*kv_copies(0, 0, 1))
    project_q(0, 1)

    x_a.wait_recv()
    start(y_fwd)
    y_b.wait_recv()
    start(x_fwd)
    x_b.wait_recv()
    y_a.wait_recv()
    project_kv(1, 2)
    start(*kv_copies(1, 1, 2))
    start(d_adj)
    project_q(1, 2)
    start(*rim_copies(1), *rim_copies(2))

    ones = jnp.ones((rows, cols), jnp.bfloat16)

    def mixing(s):
        def slot_of(c):
            c = (c + 4) % 4
            return (c % 2 + cx) % 2 + 2 * ((c // 2 + cy) % 2)

        prev_rim = rims[slot_of(slot_chip[s] - 1 + core), 1]
        next_rim = rims[slot_of(slot_chip[s] + core), 0]
        rim = jnp.concatenate([prev_rim, next_rim], 0)
        block = fall[s, :, chip_cols]
        own, pn = adj_bits[s, :rows], adj_bits[s, rows:]
        contract = (((0,), (0,)), ((), ()))
        total = block.astype(jnp.float32)
        total += jnp.dot(own, block, preferred_element_type=jnp.float32)
        total += lax.dot_general(pn, rim, contract, preferred_element_type=jnp.float32)
        degree = 1.0 + jnp.dot(own, ones, preferred_element_type=jnp.float32)
        degree += lax.dot_general(pn, ones[: 2 * band], contract, preferred_element_type=jnp.float32)
        for g in range(2):
            lhs[:, (2 + g) * cols : (3 + g) * cols] = (
                total[:, g * cols : (g + 1) * cols] / degree
            ).astype(jnp.bfloat16)

    def score_of(s, g, h, n, first, last):
        keys = kt[g * cols : (g + 1) * cols, first * rows : last * rows]
        query = qs[g, s, h * rows : (h + n) * rows]
        return jnp.dot(query, keys, preferred_element_type=jnp.float32)

    def weigh(score, state):
        peak = jnp.max(score, -1, keepdims=True)
        if state is not None:
            peak = jnp.maximum(peak, state[0])
        return peak, jnp.exp2(score - peak).astype(jnp.bfloat16)

    def gathered(g, first, last, peak, weight, state):
        total = jnp.dot(weight, v1[g, first * rows : last * rows], preferred_element_type=jnp.float32)
        if state is not None:
            total += state[1] * jnp.exp2(state[0] - peak)
        return peak, total

    def pipeline(s, first, last, states, n):
        order = [(g, h) for g in range(2) for h in range(0, heads, n)]
        scores, weights = {}, {}

        def state(g, h):
            if states is None:
                return None
            return [jnp.concatenate([states[g, h + k][e] for k in range(n)], 0) for e in range(2)]

        for k in range(len(order) + 2):
            if k < len(order):
                scores[k] = score_of(s, *order[k], n, first, last)
            if 0 <= k - 1 < len(order):
                weights[k - 1] = weigh(scores.pop(k - 1), state(*order[k - 1]))
            if k >= 2:
                g, h = order[k - 2]
                peak, total = gathered(g, first, last, *weights.pop(k - 2), state(g, h))
                for e in range(n):
                    span = slice(e * rows, (e + 1) * rows)
                    yield (g, h + e), (peak[span], total[span])

    def begin(s, last):
        return dict(pipeline(s, 0, last, None, 1))

    def finish(s, first, states, n):
        for (g, h), (_, both) in pipeline(s, first, 8, states, n):
            if h == 0:
                top = jnp.zeros((rows, cols), jnp.float32)
                bottom = jnp.ones((rows, cols), jnp.float32)
            top = jnp.where(lane_head == h, both[:, :cols], top)
            bottom = jnp.where(lane_head == h, both[:, cols:], bottom)
            if h == heads - 1:
                lhs[:, g * cols : (g + 1) * cols] = (top / bottom).astype(jnp.bfloat16)

    def project_out():
        return jnp.dot(lhs[...], w2[...], preferred_element_type=jnp.float32)

    for copy in kv_copies(0, 0, 1):
        copy.wait_recv()
    begun_x = begin(1, 4)
    begun_y = begin(2, 4)

    x_fwd.wait_recv()
    y_fwd.wait_recv()
    start(*rim_copies(3))
    start(x_adj, y_adj)
    project_kv(3, 1)
    start(*kv_copies(2, 3, 1))
    for copy in kv_copies(1, 1, 2):
        copy.wait_recv()
    project_q(3, 1)
    begun_d = begin(3, 6)

    d_adj.wait_recv()
    for s in range(4):
        for copy in rim_copies(s):
            copy.wait_recv()
    mixing(3)
    for load in loads[8:]:
        load.wait()
    for copy in w_copies[3:]:
        copy.wait_recv()

    x_relay = remote(rs_out.at[2, low], relay_in.at[0], rs_send.at[0], rs_recv.at[0], x_dev)
    y_relay = remote(rs_out.at[2, high], relay_in.at[1], rs_send.at[1], rs_recv.at[1], y_dev)
    x_low = remote(rs_out.at[0, low], rs_in.at[0, low], rs_send.at[2], rs_recv.at[2], x_dev)
    x_high = remote(rs_out.at[0, high], rs_in.at[0, high], rs_send.at[3], rs_recv.at[3], x_dev)
    y_low = remote(rs_out.at[1, low], rs_in.at[1, low], rs_send.at[4], rs_recv.at[4], y_dev)
    y_high = remote(rs_out.at[1, high], rs_in.at[1, high], rs_send.at[5], rs_recv.at[5], y_dev)

    local = jnp.dot(lhs[:, 2 * cols :], w2[2 * cols :], preferred_element_type=jnp.float32)
    for copy in kv_copies(2, 3, 1):
        copy.wait_recv()
    finish(3, 6, begun_d, 1)
    attn = jnp.dot(lhs[:, : 2 * cols], w2[: 2 * cols], preferred_element_type=jnp.float32)
    rs_out[2] = (local + attn).astype(jnp.bfloat16)
    start(x_relay, y_relay)
    finish(2, 4, begun_y, 1)
    y_adj.wait_recv()
    mixing(2)
    part = project_out()
    rs_out[1, high] = part[half:].astype(jnp.bfloat16)
    start(y_high)
    keep[1] = part[:half]
    finish(1, 4, begun_x, 1)
    x_adj.wait_recv()
    mixing(1)
    part = project_out()
    rs_out[0, low] = part[:half].astype(jnp.bfloat16)
    start(x_low)
    keep[0] = part[half:]
    mixing(0)
    finish(0, 0, None, 1)
    part = project_out() + fall[0].astype(jnp.float32)
    keep[2] = part[:half]
    keep[3] = part[half:]
    y_relay.wait_recv()
    rs_out[0, high] = (keep[0] + relay_in[1].astype(jnp.float32)).astype(jnp.bfloat16)
    start(x_high)
    x_relay.wait_recv()
    rs_out[1, low] = (keep[1] + relay_in[0].astype(jnp.float32)).astype(jnp.bfloat16)
    start(y_low)
    for copy in sent[:-2]:
        copy.wait_send()
    x_low.wait_recv()
    keep[2] += rs_in[0, low].astype(jnp.float32)
    y_high.wait_recv()
    keep[3] += rs_in[1, high].astype(jnp.float32)
    x_high.wait_recv()
    out[high] = (keep[3] + rs_in[0, high].astype(jnp.float32)).astype(out.dtype)
    y_low.wait_recv()
    out[low] = (keep[2] + rs_in[1, low].astype(jnp.float32)).astype(out.dtype)
    for copy in sent[-2:]:
        copy.wait_send()


def fused_layer(feats, adj_own, adj_prev, adj_next, bcount, wqkv, w_mp, w_out):
    rows, width = feats.shape
    cols = w_out.shape[0]
    band = adj_prev.shape[1]
    nodes = rows * lax.axis_size("dom")
    head_size = width // HEADS
    heads = cols // head_size
    vmem = pl.BlockSpec(memory_space=pltpu.VMEM)
    hbm = pl.BlockSpec(memory_space=pltpu.HBM)
    bf16, f32 = jnp.bfloat16, jnp.float32
    dma = pltpu.SemaphoreType.DMA
    operands = (feats, adj_own, adj_prev.T, adj_next.T, bcount.T, wqkv, w_mp, w_out)
    pinned = [pltpu.with_memory_space_constraint(a, pltpu.HBM) for a in operands]
    return pl.pallas_call(
        functools.partial(layer_kernel, head_size),
        out_shape=pltpu.VMEM((rows, width), bf16),
        in_specs=[hbm] * 8,
        out_specs=vmem,
        scratch_shapes=[
            pltpu.VMEM((4, rows, width), bf16),
            pltpu.VMEM(adj_own.shape, adj_own.dtype),
            pltpu.VMEM(adj_prev.shape[::-1], adj_prev.dtype),
            pltpu.VMEM(adj_next.shape[::-1], adj_next.dtype),
            pltpu.VMEM(bcount.shape[::-1], bcount.dtype),
            pltpu.VMEM((width, 6 * cols), bf16),
            pltpu.VMEM((4 * cols, width), bf16),
            pltpu.VMEM((2, 4, heads * rows, cols), bf16),
            pltpu.VMEM((2 * cols, nodes), bf16),
            pltpu.VMEM((2, nodes, 2 * cols), bf16),
            pltpu.VMEM((4, rows + 2 * band, rows), bf16),
            pltpu.VMEM((4, 2, band, 2 * cols), bf16),
            pltpu.VMEM((rows, 4 * cols), bf16),
            pltpu.VMEM((4, rows // 2, width), f32),
            pltpu.VMEM((3, rows, width), bf16),
            pltpu.VMEM((2, rows, width), bf16),
            pltpu.VMEM((2, rows // 2, width), bf16),
            dma((10,)),
            dma((19,)),
            dma((19,)),
            dma((6,)),
            dma((6,)),
            dma((3,)),
            dma((3,)),
            dma((6,)),
            dma((6,)),
        ],
        compiler_params=pltpu.CompilerParams(
            collective_id=0, has_side_effects=True, vmem_limit_bytes=40 * 1024 * 1024
        ),
    )(*pinned)


def solution(mesh):
    placed = (
        P(("dp", "dom"), None),
        P(("dp", "dom"), None),
        P(("dp", "dom"), None),
        P(("dp", "dom"), None),
        P("dp", None),
        P(None, None, "dom"),
        P("dom", None),
        P("dom", None),
    )
    layer = fused_layer if mesh.shape["dom"] == 8 else body
    return jax.shard_map(
        layer, mesh=mesh, in_specs=placed, out_specs=P(("dp", "dom"), None), check_vma=False
    )
```

```python
import functools
import math

import jax
import jax.numpy as jnp
from jax import lax
from jax.experimental import pallas as pl
from jax.experimental.pallas import tpu as pltpu
from jax.sharding import PartitionSpec as P

HEADS = 32


def with_halo(cells, sides, width):
    for axis, dim in sides:
        count = lax.axis_size(axis)
        ends = count - 1
        head = lax.slice_in_dim(cells, 0, width, axis=dim)
        tail = lax.slice_in_dim(cells, cells.shape[dim] - width, cells.shape[dim], axis=dim)
        cells = jnp.concatenate(
            [
                lax.ppermute(tail, axis, [(i, (i + 1) % count) for i in range(ends)]),
                cells,
                lax.ppermute(head, axis, [((i + 1) % count, i) for i in range(ends)]),
            ],
            axis=dim,
        )
    return cells


def attend(head_qkv, head_size):
    nodes = head_qkv.shape[1]
    columns = head_qkv.shape[2]
    count_heads = columns // head_size
    query = head_qkv[0].reshape(nodes, count_heads, head_size)
    key = head_qkv[1].reshape(nodes, count_heads, head_size)
    value = head_qkv[2].reshape(nodes, count_heads, head_size)
    scale = 1.0 / head_size**0.5
    block = math.gcd(nodes, 512)

    def one_block(index):
        q_block = lax.dynamic_slice_in_dim(query, index * block, block, 0)
        score = jnp.einsum("qhc,khc->hqk", q_block, key, preferred_element_type=jnp.float32) * scale
        peak = jnp.max(score, -1, keepdims=True)
        expo = jnp.exp(score - peak)
        weight = (expo / jnp.sum(expo, -1, keepdims=True)).astype(jnp.bfloat16)
        result = jnp.einsum("hqk,khc->qhc", weight, value, preferred_element_type=jnp.float32)
        return result.astype(jnp.bfloat16).reshape(block, columns)

    blocks = lax.map(one_block, jnp.arange(nodes // block))
    return blocks.reshape(nodes, columns)


def message_term(mixed, w_mp):
    return jnp.dot(
        mixed, lax.all_gather(w_mp, "dom", axis=0, tiled=True), preferred_element_type=jnp.float32
    )


def body(feats, adj_own, adj_prev, adj_next, bcount, wqkv, w_mp, w_out):
    rows = feats.shape[0]
    width = feats.shape[1]
    band = adj_prev.shape[1]
    parts = lax.axis_size("dom")
    myself = lax.axis_index("dom")
    padded = with_halo(feats, (("dom", 0),), band)
    prev_rim = padded[:band]
    next_rim = padded[band + rows :]
    column = jnp.arange(band)
    prev_count = bcount[jnp.maximum(myself - 1, 0), 1]
    next_count = bcount[jnp.minimum(myself + 1, parts - 1), 0]
    prev_vis = (myself > 0) & (column >= band - prev_count)
    next_vis = (myself < parts - 1) & (column < next_count)
    own = adj_own.astype(jnp.bfloat16)
    prv = jnp.where(prev_vis[None, :], adj_prev, 0).astype(jnp.bfloat16)
    nxt = jnp.where(next_vis[None, :], adj_next, 0).astype(jnp.bfloat16)
    degree = (
        1.0
        + jnp.sum(own.astype(jnp.float32), -1)
        + jnp.sum(prv.astype(jnp.float32), -1)
        + jnp.sum(nxt.astype(jnp.float32), -1)
    )
    total = feats.astype(jnp.float32) + jnp.dot(own, feats, preferred_element_type=jnp.float32)
    total = total + jnp.dot(prv, prev_rim, preferred_element_type=jnp.float32)
    total = total + jnp.dot(nxt, next_rim, preferred_element_type=jnp.float32)
    mixed = (total / degree[:, None]).astype(jnp.bfloat16)
    node_qkv = jnp.einsum(
        "nd,tdc->tnc",
        feats,
        lax.all_gather(wqkv, "dom", axis=2, tiled=True),
        preferred_element_type=jnp.float32,
    ).astype(jnp.bfloat16)
    head_qkv = lax.all_to_all(node_qkv, "dom", split_axis=2, concat_axis=1, tiled=True)
    head_out = attend(head_qkv, width // HEADS)
    node_out = lax.all_to_all(head_out, "dom", split_axis=0, concat_axis=1, tiled=True)
    local = message_term(mixed, w_mp)
    attn = jnp.dot(
        node_out,
        lax.all_gather(w_out, "dom", axis=0, tiled=True),
        preferred_element_type=jnp.float32,
    )
    return (feats.astype(jnp.float32) + local + attn).astype(jnp.bfloat16)


def layer_kernel(
    head_size,
    feats, adj_own, adj_prev, adj_next, bcount, wqkv, w_mp, w_out, out,
    fall, own_adj, prev_adj, next_adj, counts, wcat, w2, qs, kt, v1, adj_bits, rims, lhs,
    keep, rs_out, rs_in, relay_in,
    load_sem, sib_send, sib_recv, ag_send, ag_recv, adj_send, adj_recv, rs_send, rs_recv,
):
    rows, width = feats.shape
    cols = w_out.shape[0]
    band = adj_prev.shape[0]
    half = rows // 2
    heads = cols // head_size
    parts = counts.shape[1]
    me = lax.axis_index("dom")
    core = me % 2
    chip = me // 2
    sib = me + 1 - 2 * core
    cx, cy = chip % 2, chip // 2
    slot_chip = [cy * 2 + cx, cy * 2 + 1 - cx, (1 - cy) * 2 + cx, (1 - cy) * 2 + 1 - cx]
    x_dev, y_dev, d_dev = [slot_chip[k] * 2 + core for k in (1, 2, 3)]
    mesh_id = pl.DeviceIdType.MESH

    def remote(src, dst, send_sem, recv_sem, dev):
        return pltpu.make_async_remote_copy(
            src_ref=src, dst_ref=dst, send_sem=send_sem, recv_sem=recv_sem,
            device_id={"dom": dev}, device_id_type=mesh_id,
        )

    def col_at(k):
        return pl.ds(pl.multiple_of(k * cols, cols), cols)

    pairs = [(feats, fall.at[0])]
    pairs += [(wqkv.at[t], wcat.at[:, col_at(2 * t + core)]) for t in range(3)]
    pairs += [(adj_own, own_adj), (adj_prev, prev_adj), (adj_next, next_adj), (bcount, counts)]
    pairs += [(w_out, w2.at[col_at(core)]), (w_mp, w2.at[col_at(2 + core)])]
    loads = [pltpu.make_async_copy(a, b, load_sem.at[k]) for k, (a, b) in enumerate(pairs)]
    for load in loads:
        load.start()

    barrier = pltpu.get_barrier_semaphore()
    for dev in (x_dev, y_dev, sib):
        pl.semaphore_signal(barrier, inc=1, device_id={"dom": dev}, device_id_type=mesh_id)
    pl.semaphore_wait(barrier, 3)

    low, high = pl.ds(0, half), pl.ds(half, half)

    def gather(k, src, slot, span, dev):
        return remote(src, fall.at[slot, span], ag_send.at[k], ag_recv.at[k], dev)

    x_a = gather(0, feats.at[low], 1, low, x_dev)
    y_b = gather(1, feats.at[high], 2, high, y_dev)
    x_b = gather(2, feats.at[high], 1, high, x_dev)
    y_a = gather(3, feats.at[low], 2, low, y_dev)
    x_fwd = gather(4, fall.at[2, high], 3, high, x_dev)
    y_fwd = gather(5, fall.at[1, low], 3, low, y_dev)
    w_copies = [
        remote(wqkv.at[t], wcat.at[:, col_at(2 * t + core)], sib_send.at[t], sib_recv.at[t], sib)
        for t in range(3)
    ]
    w_copies += [
        remote(w_out, w2.at[col_at(core)], sib_send.at[3], sib_recv.at[3], sib),
        remote(w_mp, w2.at[col_at(2 + core)], sib_send.at[4], sib_recv.at[4], sib),
    ]
    chip_cols = pl.ds(pl.multiple_of(chip * 2 * cols, 2 * cols), 2 * cols)

    def rim_copies(s):
        return [
            remote(
                fall.at[s, pl.ds(e * (rows - band), band), chip_cols], rims.at[s, e],
                sib_send.at[5 + 2 * s + e], sib_recv.at[5 + 2 * s + e], sib,
            )
            for e in range(2)
        ]

    def key_at(s, theirs=False):
        return (6 * rows if s == 3 else s * rows) + theirs * (rows if s == 3 else 3 * rows)

    def kv_copies(k, s, n):
        own, theirs = pl.ds(key_at(s), n * rows), pl.ds(key_at(s, True), n * rows)
        lanes = pl.ds(0, cols)
        return [
            remote(kt.at[:, own], kt.at[:, theirs], sib_send.at[13 + 2 * k], sib_recv.at[13 + 2 * k], sib),
            remote(
                v1.at[:, own, lanes], v1.at[:, theirs, lanes],
                sib_send.at[14 + 2 * k], sib_recv.at[14 + 2 * k], sib,
            ),
        ]

    x_adj, y_adj, d_adj = [
        remote(adj_bits.at[0], adj_bits.at[k + 1], adj_send.at[k], adj_recv.at[k], dev)
        for k, dev in enumerate((x_dev, y_dev, d_dev))
    ]

    sent = []

    def start(*copies):
        for copy in copies:
            copy.start()
            sent.append(copy)

    start(x_a, y_b, *w_copies[:3], x_b, y_a, *w_copies[3:])

    v1[:, :, cols:] = jnp.ones_like(v1[:, :, cols:])
    lane_head = lax.broadcasted_iota(jnp.int32, (1, cols), 1) // head_size
    factor = math.log2(math.e) / head_size**0.5

    def project(s, n):
        block = fall[s] if n == 1 else fall[s : s + n].reshape(n * rows, width)
        r = jnp.dot(block, wcat[...], preferred_element_type=jnp.float32)
        for g in range(2):
            for i in range(n):
                q = r[i * rows : (i + 1) * rows, g * cols : (g + 1) * cols] * factor
                for h in range(heads):
                    qs[g, s + i, h * rows : (h + 1) * rows, :] = jnp.where(lane_head == h, q, 0.0).astype(
                        jnp.bfloat16
                    )
            v1[g, key_at(s) : key_at(s) + n * rows, :cols] = r[:, (4 + g) * cols : (5 + g) * cols].astype(
                jnp.bfloat16
            )
        kt[:, key_at(s) : key_at(s) + n * rows] = r[:, 2 * cols : 4 * cols].T.astype(jnp.bfloat16)

    def project_kv(s):
        r = jnp.dot(fall[s], wcat[:, 2 * cols :], preferred_element_type=jnp.float32)
        first = key_at(s)
        for g in range(2):
            v1[g, first : first + rows, :cols] = r[:, (2 + g) * cols : (3 + g) * cols].astype(jnp.bfloat16)
        kt[:, first : first + rows] = r[:, : 2 * cols].T.astype(jnp.bfloat16)

    def project_q(s):
        r = jnp.dot(fall[s], wcat[:, : 2 * cols], preferred_element_type=jnp.float32)
        for g in range(2):
            q = r[:, g * cols : (g + 1) * cols] * factor
            for h in range(heads):
                qs[g, s, h * rows : (h + 1) * rows, :] = jnp.where(lane_head == h, q, 0.0).astype(
                    jnp.bfloat16
                )

    for load in loads[4:8]:
        load.wait()
    before, after = (me + parts - 1) % parts, (me + 1) % parts
    column = lax.broadcasted_iota(jnp.int32, (band, 1), 0)
    device = lax.broadcasted_iota(jnp.int32, (1, parts), 1)
    prev_count = jnp.sum(jnp.where((device == before) & (me > 0), counts[1:2], 0), -1, keepdims=True)
    next_count = jnp.sum(
        jnp.where((device == after) & (me < parts - 1), counts[0:1], 0), -1, keepdims=True
    )
    adj_bits[0, :rows] = own_adj[...].astype(jnp.float32).astype(jnp.bfloat16)
    adj_bits[0, rows : rows + band] = (
        jnp.where(column >= band - prev_count, prev_adj[...], 0).astype(jnp.float32).astype(jnp.bfloat16)
    )
    adj_bits[0, rows + band :] = (
        jnp.where(column < next_count, next_adj[...], 0).astype(jnp.float32).astype(jnp.bfloat16)
    )

    for load in loads[:4]:
        load.wait()
    start(*rim_copies(0))
    for copy in w_copies[:3]:
        copy.wait_recv()
    project(0, 1)
    start(*kv_copies(0, 0, 1))

    x_a.wait_recv()
    start(y_fwd)
    y_b.wait_recv()
    start(x_fwd)
    x_b.wait_recv()
    y_a.wait_recv()
    project(1, 2)
    start(*kv_copies(1, 1, 2))
    start(d_adj)
    start(*rim_copies(1), *rim_copies(2))

    ones = jnp.ones((rows, cols), jnp.bfloat16)

    def mixing(s):
        def slot_of(c):
            c = (c + 4) % 4
            return (c % 2 + cx) % 2 + 2 * ((c // 2 + cy) % 2)

        prev_rim = rims[slot_of(slot_chip[s] - 1 + core), 1]
        next_rim = rims[slot_of(slot_chip[s] + core), 0]
        rim = jnp.concatenate([prev_rim, next_rim], 0)
        block = fall[s, :, chip_cols]
        own, pn = adj_bits[s, :rows], adj_bits[s, rows:]
        contract = (((0,), (0,)), ((), ()))
        total = block.astype(jnp.float32)
        total += jnp.dot(own, block, preferred_element_type=jnp.float32)
        total += lax.dot_general(pn, rim, contract, preferred_element_type=jnp.float32)
        degree = 1.0 + jnp.dot(own, ones, preferred_element_type=jnp.float32)
        degree += lax.dot_general(pn, ones[: 2 * band], contract, preferred_element_type=jnp.float32)
        for g in range(2):
            lhs[:, (2 + g) * cols : (3 + g) * cols] = (
                total[:, g * cols : (g + 1) * cols] / degree
            ).astype(jnp.bfloat16)

    def score_of(s, g, h, n, first, last):
        keys = kt[g * cols : (g + 1) * cols, first * rows : last * rows]
        query = qs[g, s, h * rows : (h + n) * rows]
        return jnp.dot(query, keys, preferred_element_type=jnp.float32)

    def weigh(score, state):
        peak = jnp.max(score, -1, keepdims=True)
        if state is not None:
            peak = jnp.maximum(peak, state[0])
        return peak, jnp.exp2(score - peak).astype(jnp.bfloat16)

    def gathered(g, first, last, peak, weight, state):
        total = jnp.dot(weight, v1[g, first * rows : last * rows], preferred_element_type=jnp.float32)
        if state is not None:
            total += state[1] * jnp.exp2(state[0] - peak)
        return peak, total

    def pipeline(s, first, last, states, n):
        order = [(g, h) for g in range(2) for h in range(0, heads, n)]
        scores, weights = {}, {}

        def state(g, h):
            if states is None:
                return None
            return [jnp.concatenate([states[g, h + k][e] for k in range(n)], 0) for e in range(2)]

        for k in range(len(order) + 2):
            if k < len(order):
                scores[k] = score_of(s, *order[k], n, first, last)
            if 0 <= k - 1 < len(order):
                weights[k - 1] = weigh(scores.pop(k - 1), state(*order[k - 1]))
            if k >= 2:
                g, h = order[k - 2]
                peak, total = gathered(g, first, last, *weights.pop(k - 2), state(g, h))
                for e in range(n):
                    span = slice(e * rows, (e + 1) * rows)
                    yield (g, h + e), (peak[span], total[span])

    def begin(s, last):
        return dict(pipeline(s, 0, last, None, 1))

    def finish(s, first, states, n):
        for (g, h), (_, both) in pipeline(s, first, 8, states, n):
            if h == 0:
                top = jnp.zeros((rows, cols), jnp.float32)
                bottom = jnp.ones((rows, cols), jnp.float32)
            top = jnp.where(lane_head == h, both[:, :cols], top)
            bottom = jnp.where(lane_head == h, both[:, cols:], bottom)
            if h == heads - 1:
                lhs[:, g * cols : (g + 1) * cols] = (top / bottom).astype(jnp.bfloat16)

    def project_out():
        return jnp.dot(lhs[...], w2[...], preferred_element_type=jnp.float32)

    for copy in kv_copies(0, 0, 1):
        copy.wait_recv()
    begun_x = begin(1, 4)
    begun_y = begin(2, 4)

    x_fwd.wait_recv()
    y_fwd.wait_recv()
    start(*rim_copies(3))
    start(x_adj, y_adj)
    project_kv(3)
    start(*kv_copies(2, 3, 1))
    for copy in kv_copies(1, 1, 2):
        copy.wait_recv()
    project_q(3)
    begun_d = begin(3, 6)

    d_adj.wait_recv()
    for s in range(4):
        for copy in rim_copies(s):
            copy.wait_recv()
    mixing(3)
    for load in loads[8:]:
        load.wait()
    for copy in w_copies[3:]:
        copy.wait_recv()

    x_relay = remote(rs_out.at[2, low], relay_in.at[0], rs_send.at[0], rs_recv.at[0], x_dev)
    y_relay = remote(rs_out.at[2, high], relay_in.at[1], rs_send.at[1], rs_recv.at[1], y_dev)
    x_low = remote(rs_out.at[0, low], rs_in.at[0, low], rs_send.at[2], rs_recv.at[2], x_dev)
    x_high = remote(rs_out.at[0, high], rs_in.at[0, high], rs_send.at[3], rs_recv.at[3], x_dev)
    y_low = remote(rs_out.at[1, low], rs_in.at[1, low], rs_send.at[4], rs_recv.at[4], y_dev)
    y_high = remote(rs_out.at[1, high], rs_in.at[1, high], rs_send.at[5], rs_recv.at[5], y_dev)

    local = jnp.dot(lhs[:, 2 * cols :], w2[2 * cols :], preferred_element_type=jnp.float32)
    for copy in kv_copies(2, 3, 1):
        copy.wait_recv()
    finish(3, 6, begun_d, 1)
    attn = jnp.dot(lhs[:, : 2 * cols], w2[: 2 * cols], preferred_element_type=jnp.float32)
    rs_out[2] = (local + attn).astype(jnp.bfloat16)
    start(x_relay, y_relay)
    finish(2, 4, begun_y, 1)
    y_adj.wait_recv()
    mixing(2)
    part = project_out()
    rs_out[1, high] = part[half:].astype(jnp.bfloat16)
    start(y_high)
    keep[1] = part[:half]
    finish(1, 4, begun_x, 1)
    x_adj.wait_recv()
    mixing(1)
    part = project_out()
    rs_out[0, low] = part[:half].astype(jnp.bfloat16)
    start(x_low)
    keep[0] = part[half:]
    mixing(0)
    finish(0, 0, None, 1)
    part = project_out() + fall[0].astype(jnp.float32)
    keep[2] = part[:half]
    keep[3] = part[half:]
    y_relay.wait_recv()
    rs_out[0, high] = (keep[0] + relay_in[1].astype(jnp.float32)).astype(jnp.bfloat16)
    start(x_high)
    x_relay.wait_recv()
    rs_out[1, low] = (keep[1] + relay_in[0].astype(jnp.float32)).astype(jnp.bfloat16)
    start(y_low)
    x_low.wait_recv()
    keep[2] += rs_in[0, low].astype(jnp.float32)
    y_high.wait_recv()
    keep[3] += rs_in[1, high].astype(jnp.float32)
    x_high.wait_recv()
    out[high] = (keep[3] + rs_in[0, high].astype(jnp.float32)).astype(out.dtype)
    y_low.wait_recv()
    out[low] = (keep[2] + rs_in[1, low].astype(jnp.float32)).astype(out.dtype)
    for copy in sent:
        copy.wait_send()


def fused_layer(feats, adj_own, adj_prev, adj_next, bcount, wqkv, w_mp, w_out):
    rows, width = feats.shape
    cols = w_out.shape[0]
    band = adj_prev.shape[1]
    nodes = rows * lax.axis_size("dom")
    head_size = width // HEADS
    heads = cols // head_size
    vmem = pl.BlockSpec(memory_space=pltpu.VMEM)
    hbm = pl.BlockSpec(memory_space=pltpu.HBM)
    bf16, f32 = jnp.bfloat16, jnp.float32
    dma = pltpu.SemaphoreType.DMA
    operands = (feats, adj_own, adj_prev.T, adj_next.T, bcount.T, wqkv, w_mp, w_out)
    pinned = [pltpu.with_memory_space_constraint(a, pltpu.HBM) for a in operands]
    return pl.pallas_call(
        functools.partial(layer_kernel, head_size),
        out_shape=pltpu.VMEM((rows, width), bf16),
        in_specs=[hbm] * 8,
        out_specs=vmem,
        scratch_shapes=[
            pltpu.VMEM((4, rows, width), bf16),
            pltpu.VMEM(adj_own.shape, adj_own.dtype),
            pltpu.VMEM(adj_prev.shape[::-1], adj_prev.dtype),
            pltpu.VMEM(adj_next.shape[::-1], adj_next.dtype),
            pltpu.VMEM(bcount.shape[::-1], bcount.dtype),
            pltpu.VMEM((width, 6 * cols), bf16),
            pltpu.VMEM((4 * cols, width), bf16),
            pltpu.VMEM((2, 4, heads * rows, cols), bf16),
            pltpu.VMEM((2 * cols, nodes), bf16),
            pltpu.VMEM((2, nodes, 2 * cols), bf16),
            pltpu.VMEM((4, rows + 2 * band, rows), bf16),
            pltpu.VMEM((4, 2, band, 2 * cols), bf16),
            pltpu.VMEM((rows, 4 * cols), bf16),
            pltpu.VMEM((4, rows // 2, width), f32),
            pltpu.VMEM((3, rows, width), bf16),
            pltpu.VMEM((2, rows, width), bf16),
            pltpu.VMEM((2, rows // 2, width), bf16),
            dma((10,)),
            dma((19,)),
            dma((19,)),
            dma((6,)),
            dma((6,)),
            dma((3,)),
            dma((3,)),
            dma((6,)),
            dma((6,)),
        ],
        compiler_params=pltpu.CompilerParams(
            collective_id=0, has_side_effects=True, vmem_limit_bytes=40 * 1024 * 1024
        ),
    )(*pinned)


def solution(mesh):
    placed = (
        P(("dp", "dom"), None),
        P(("dp", "dom"), None),
        P(("dp", "dom"), None),
        P(("dp", "dom"), None),
        P("dp", None),
        P(None, None, "dom"),
        P("dom", None),
        P("dom", None),
    )
    layer = fused_layer if mesh.shape["dom"] == 8 else body
    return jax.shard_map(
        layer, mesh=mesh, in_specs=placed, out_specs=P(("dp", "dom"), None), check_vma=False
    )
```
